32 devices in a mesh: groups: 1, expert: 32 (over z, y, x, core).
Axes of the slice: x: 2, y: 2, z: 4, core: 2. Of those that a mesh axis runs over, the one named last changes fastest.
Arguments:
- hidden_rows: bfloat16 [2, 256, 4096], P(None, ('groups', 'expert')), may hold values from -6 to 6
- expert_ids: int32 [2, 256, 8], P(None, ('groups', 'expert')), may hold values from 0 to 15, all different within a row; in each aligned block of 8 rows (0 to 7, 8 to 15, ..., all dimensions but the last counted through in order) at most 8 rows name the same one
- gate_codes: int32 [2, 256, 8], P(None, ('groups', 'expert')), may hold values from 1 to 1023
- gate_weight: bfloat16 [4096, 16384], P(None, 'expert'), may hold values from -0.09375 to 0.09375
- up_weight: bfloat16 [4096, 16384], P(None, 'expert'), may hold values from -0.09375 to 0.09375
- down_weight: bfloat16 [16384, 4096], P('expert'), may hold values from -0.1875 to 0.1875
Outputs:
- combined: bfloat16 [2, 256, 4096], P(None, ('groups', 'expert'))
The draws below stay inside these ranges and needn't reach their ends.
Inputs may be any that keep to these rules, and one draw needn't show every extreme that they name: `expert_ids`: each row names 8 different experts; in each decode step no expert is named by more than 8 of the rows of one device, a bound that some block reaches.
All inputs are finite; a program needn't handle non-finite values.
Results may differ from the reference program's by a relative error of at most 0.0085.
Values may be sent and summed in bfloat16 or wider, within the bound.
A program may use at most 64 MiB of HBM per device.

```python
import math
import jax
import jax.numpy as jnp
import numpy as np
from jax import lax

DW = 4096
HW = 1024
TOP = 8
MICRO = 2
RD = 8
HALF = 512
EXPERTS = 16
ROWS = 256
MOST = 8
N_EXPERT = 32


def plant(entries, own_key, smallest, high):
    shape = entries.shape
    index_at = [jax.random.randint(jax.random.fold_in(own_key, axis), (), 0, shape[axis]) for axis in range(len(shape))]
    entries = entries.at[tuple(index_at)].set(smallest)
    longest = shape.index(max(shape))
    index_at[longest] = (index_at[longest] + 1) % shape[longest]
    return entries.at[tuple(index_at)].set(high)


def block_scale(rng, shape, split, least, largest):
    level = 1.0
    for axis_at, parts in split:
        draws = jax.random.uniform(jax.random.fold_in(jax.random.fold_in(rng, 6), axis_at), (parts,), jnp.float32, least / len(split), largest / len(split))
        level = level * jnp.repeat(jnp.exp(draws), shape[axis_at] // parts).reshape((-1,) + (1,) * (len(shape) - 1 - axis_at))
    return level


def routed_block(own_key, own, number, rows, count, top, bound, slope):
    sequence = jax.random.permutation(own_key, count)
    packed, ordinary = shares(count, rows * top, bound, slope, True), shares(count, rows * top, bound, slope, False)
    places = jnp.arange(count)

    def named(lengths, turn):
        used = int((lengths > 0).sum())
        fixed = max(1, used // 4)
        passed = fixed + (places - fixed + turn * (used - fixed)) % max(1, count - fixed)
        return jnp.zeros((count,), jnp.int32).at[sequence[jnp.where(places < fixed, places, passed)]].set(jnp.asarray(lengths, jnp.int32))

    lengths = jnp.where(number % 4 == 0, named(packed, number // 4), named(ordinary, number - number // 4 - 1))
    mixed = jax.random.permutation(jax.random.fold_in(own, 3), count)
    donor, receiver = mixed[0:count // 2 * 2:2], mixed[1:count // 2 * 2:2]
    margin = jnp.minimum(lengths[donor] - 1, bound - lengths[receiver]) // 2
    margin = jnp.where((donor == sequence[0]) | (receiver == sequence[0]) | (lengths[receiver] == 0), 0, jnp.maximum(margin, 0))
    passed = jax.random.randint(jax.random.fold_in(own, 4), (count // 2,), 0, 1 << 20) % (margin + 1)
    lengths = lengths.at[donor].add(-passed).at[receiver].add(passed)
    members = jnp.searchsorted(jnp.cumsum(lengths), jnp.arange(rows * top), side="right").astype(jnp.int32)
    table = members.reshape(top, rows).T
    table = table[jax.random.permutation(jax.random.fold_in(own, 1), rows)]
    turn = jax.random.randint(jax.random.fold_in(own, 2), (rows, 1), 0, top)
    return jnp.take_along_axis(table, (jnp.arange(top)[None, :] + turn) % top, axis=1)


def shares(amount, total, most, slope, full):
    weights = [(1 << 20) // math.isqrt(grade ** slope) + 1 for grade in range(1, amount + 1)]
    largest = most if full else min(most, max(-(-total // amount), total * weights[0] // sum(weights)))
    least = 1 if total - largest >= amount - 1 else 0
    counts, spare = [largest] + [least] * (amount - 1), total - largest - least * (amount - 1)
    while spare > 0:
        candidates = [i for i in range(1, amount) if counts[i] < largest] or [i for i in range(1, amount) if counts[i] < most]
        mass, left = sum([weights[i] for i in candidates]), spare
        for i in candidates:
            more = min(most - counts[i], max(1, left * weights[i] // mass), spare)
            counts[i] = counts[i] + more
            spare = spare - more
    return np.array(counts)


def noise(key, extent, deviation, bound, cuts=(), kind=jnp.bfloat16):
    drawn = deviation * jax.random.normal(key, extent, jnp.float32)
    if cuts:
        drawn = drawn * block_scale(key, extent, cuts, -0.22, 0.18)
    return jnp.clip(drawn, -bound, bound).astype(kind)


def setup_inputs(seed: int = 0, part: int = 0) -> dict:
    arg_keys = jax.random.split(jax.random.key(seed), 7)
    own_keys = jax.random.split(jax.random.fold_in(arg_keys[6], part), 7)
    hidden_rows = noise(own_keys[0], (MICRO, ROWS, DW), 1.0, 6.0, ((1, 32),))
    expert_ids_keys = jax.random.split(jax.random.fold_in(own_keys[1], 1), MICRO * ROWS // RD)
    expert_ids_turns = jax.random.permutation(jax.random.fold_in(own_keys[1], 3), MICRO * ROWS // RD)
    expert_ids = jax.vmap(lambda own, number: routed_block(jax.random.fold_in(own_keys[1], 2), own, number, RD, EXPERTS, TOP, MOST, 2))(expert_ids_keys, expert_ids_turns).reshape((MICRO, ROWS, TOP))
    gate_codes = plant(jax.random.randint(own_keys[2], (MICRO, ROWS, TOP), 1, 1024), jax.random.fold_in(own_keys[2], 1), 1, 1023).astype(jnp.int32)
    gate_weight = noise(arg_keys[3], (DW, EXPERTS * HW), DW ** -0.5, 0.09375, ((1, 32),))
    up_weight = noise(arg_keys[4], (DW, EXPERTS * HW), DW ** -0.5, 0.09375, ((1, 32),))
    down_weight = noise(arg_keys[5], (EXPERTS * HW, DW), HW ** -0.5, 0.1875, ((0, 32),))
    return dict(hidden_rows=hidden_rows, expert_ids=expert_ids, gate_codes=gate_codes, gate_weight=gate_weight, up_weight=up_weight, down_weight=down_weight)


route_scale = 2.5


def half_expert(step_rows, gate_half, up_half, down_half):
    gate_value = jnp.dot(step_rows, gate_half, preferred_element_type=jnp.float32)
    up_value = jnp.dot(step_rows, up_half, preferred_element_type=jnp.float32)
    hidden = (jax.nn.silu(gate_value) * up_value).astype(jnp.bfloat16)
    return jnp.dot(hidden, down_half, preferred_element_type=jnp.float32).astype(jnp.bfloat16)


def reference(hidden_rows, expert_ids, gate_codes, gate_weight, up_weight, down_weight):
    outputs = []
    capacity = N_EXPERT * MOST
    for micro_index in range(MICRO):
        step_rows = hidden_rows[micro_index]
        row_total = step_rows.shape[0]
        feature_count = step_rows.shape[1]
        flat_ids = expert_ids[micro_index].reshape(-1).astype(jnp.int32)
        pick_total = flat_ids.shape[0]
        padded_rows = jnp.concatenate([step_rows, jnp.zeros((1, feature_count), jnp.bfloat16)], axis=0)

        def per_expert(carried, expert_index):
            chosen = jnp.nonzero(flat_ids == expert_index, size=capacity, fill_value=pick_total)[0].astype(jnp.int32)
            picked_rows = padded_rows[chosen // TOP]
            halves = []
            for half_index in range(2):
                col_start = expert_index * HW + half_index * HALF
                gate_half = lax.dynamic_slice_in_dim(gate_weight, col_start, HALF, 1)
                up_half = lax.dynamic_slice_in_dim(up_weight, col_start, HALF, 1)
                down_half = lax.dynamic_slice_in_dim(down_weight, col_start, HALF, 0)
                halves.append(half_expert(picked_rows, gate_half, up_half, down_half).astype(jnp.float32))
            block_value = (halves[0] + halves[1]).astype(jnp.bfloat16)
            return carried.at[chosen].set(block_value, mode="drop"), None

        initial = jnp.zeros((pick_total, feature_count), jnp.bfloat16)
        expert_range = jnp.arange(EXPERTS, dtype=jnp.int32)
        gathered, _ = lax.scan(per_expert, initial, expert_range)
        picked = gathered.reshape(row_total, TOP, feature_count).astype(jnp.float32)
        code_rows = gate_codes[micro_index].astype(jnp.float32)
        weights = route_scale * code_rows / jnp.sum(code_rows, axis=1, keepdims=True)
        outputs.append(jnp.sum(weights[:, :, None] * picked, axis=1).astype(jnp.bfloat16))
    return jnp.stack(outputs, axis=0)
```

```python
import jax
import jax.numpy as jnp
from jax import lax
from jax.sharding import PartitionSpec as P

route_scale = 2.5


def dense_gates(id_block, code_block, expert_count):
    code_rows = code_block.astype(jnp.float32)
    weights = route_scale * code_rows / jnp.sum(code_rows, axis=-1, keepdims=True)
    hit = id_block[..., None] == jnp.arange(expert_count, dtype=jnp.int32)
    return jnp.sum(jnp.where(hit, weights[..., None], 0.0), axis=-2)


def shards(hidden_rows, expert_ids, gate_codes, gate_weight, up_weight, down_weight):
    peer_count = lax.axis_size("expert")
    expert_count = peer_count // 2
    micro_count, rows_dev, feature_count = hidden_rows.shape
    own_expert = lax.axis_index("expert") // 2
    gates = dense_gates(expert_ids, gate_codes, expert_count)
    all_gates = lax.all_gather(gates.reshape(micro_count * rows_dev, expert_count), "expert")
    all_rows = lax.all_gather(
        hidden_rows.reshape(micro_count * rows_dev, feature_count), "expert", tiled=True
    )
    own_gate = lax.dynamic_index_in_dim(all_gates, own_expert, 2, keepdims=False).reshape(-1, 1)
    gate_value = jnp.dot(all_rows, gate_weight, preferred_element_type=jnp.float32)
    up_value = jnp.dot(all_rows, up_weight, preferred_element_type=jnp.float32)
    hidden = (jax.nn.silu(gate_value) * up_value).astype(jnp.bfloat16)
    produced = jnp.dot(hidden, down_weight, preferred_element_type=jnp.float32)
    weighted = (produced * own_gate).astype(jnp.bfloat16)
    combined = lax.psum_scatter(weighted, "expert", scatter_dimension=0, tiled=True)
    return combined.reshape(micro_count, rows_dev, feature_count)


def solution(mesh):
    return jax.shard_map(
        shards,
        mesh=mesh,
        in_specs=(
            P(None, ("groups", "expert"), None),
            P(None, ("groups", "expert"), None),
            P(None, ("groups", "expert"), None),
            P(None, "expert"),
            P(None, "expert"),
            P("expert", None),
        ),
        out_specs=P(None, ("groups", "expert"), None),
        check_vma=False,
    )
```

```python
import functools

import jax
import jax.numpy as jnp
from jax import lax
from jax.experimental import pallas as pl
from jax.experimental.pallas import tpu as pltpu
from jax.sharding import PartitionSpec as P

route_scale = 2.5
LANES = 128


def place(n):
    me = lax.axis_index("expert")
    core, x, y, z = me % 2, (me // 2) % 2, (me // 4) % 2, me // 8
    to_y, to_x = me + 4 - 8 * y, me + 2 - 4 * x
    return dict(
        me=me, core=core, z=z, lines=n // 8,
        near=to_y * (1 - core) + to_x * core,
        far=to_x * (1 - core) + to_y * core,
        twin=me + 1 - 2 * core,
        i1=y * (1 - core) + x * core,
        i2=x * (1 - core) + y * core,
    )


def greet(at):
    barrier = pltpu.get_barrier_semaphore()
    z, lines = at["z"], at["lines"]

    def signal(device):
        pl.semaphore_signal(
            barrier, inc=1, device_id={"expert": device},
            device_id_type=pl.DeviceIdType.MESH,
        )

    for name in ("near", "far", "twin"):
        signal(at[name])

    @pl.when(z > 0)
    def _():
        signal(at["me"] - 8)

    @pl.when(z < lines - 1)
    def _():
        signal(at["me"] + 8)

    on_line = (z + lines - 1) // lines + (2 * lines - 2 - z) // lines
    pl.semaphore_wait(barrier, 3 + on_line)


def remote(src, dst, send_sem, recv_sem, device):
    return pltpu.make_async_remote_copy(
        src_ref=src, dst_ref=dst, send_sem=send_sem, recv_sem=recv_sem,
        device_id={"expert": device}, device_id_type=pl.DeviceIdType.MESH,
    )


def gather_kernel(n, own_ref, out_ref, send_sem, recv_sem):
    at = place(n)
    me, z, lines = at["me"], at["z"], at["lines"]
    near, far, twin = at["near"], at["far"], at["twin"]
    both = near + far - me
    greet(at)

    def send(kind, source, device, begin, first=False):
        copy = remote(
            own_ref if first else out_ref.at[source], out_ref.at[source],
            send_sem.at[kind, source], recv_sem.at[source], device,
        )
        if begin:
            copy.start()
        else:
            copy.wait_send()

    def arrived(source):
        remote(
            out_ref.at[source], out_ref.at[source],
            send_sem.at[0, source], recv_sem.at[source], twin,
        ).wait_recv()

    def line_sends(source, begin, up, down, first=False):
        if up:
            @pl.when(z < lines - 1)
            def _():
                send(0, source, me + 8, begin, first)
        if down:
            @pl.when(z > 0)
            def _():
                send(1, source, me - 8, begin, first)
        send(2, source, near, begin, first)
        send(3, source, far, begin, first)
        send(4, source, twin, begin, first)

    def line_step(k, begin):
        @pl.when(z >= k)
        def _():
            if begin:
                arrived(me - 8 * k)
            line_sends(me - 8 * k, begin, True, False)

        @pl.when(z + k < lines)
        def _():
            if begin:
                arrived(me + 8 * k)
            line_sends(me + 8 * k, begin, False, True)

    def side_step(base, k, to_far, begin):
        def one(source):
            if begin:
                arrived(source)
            if to_far:
                send(3, source, far, begin)
            send(4, source, twin, begin)

        if k == 0:
            one(base)
            return

        @pl.when(z >= k)
        def _():
            one(base - 8 * k)

        @pl.when(z + k < lines)
        def _():
            one(base + 8 * k)

    line_sends(me, True, True, True, True)
    out_ref[me] = own_ref[...]
    for k in range(1, lines + 3):
        if k < lines:
            line_step(k, True)
        if k - 1 < lines:
            side_step(near, k - 1, True, True)
        if 0 <= k - 2 < lines:
            side_step(far, k - 2, False, True)
        if 0 <= k - 3 < lines:
            side_step(both, k - 3, False, True)
    for chip in range(n // 2):
        arrived(2 * chip + 1 - at["core"])
    line_sends(me, False, True, True, True)
    for k in range(lines):
        if k > 0:
            line_step(k, False)
        side_step(near, k, True, False)
        side_step(far, k, False, False)
        side_step(both, k, False, False)


def scatter_kernel(
    n, part_ref, out_ref, twin_in, far_in, near_in, down_in, up_in, out_far, out_near, out_line,
    twin_send, twin_recv, far_send, far_recv, near_send, near_recv,
    down_send, down_recv, up_send, up_recv,
):
    at = place(n)
    me, z, lines, core = at["me"], at["z"], at["lines"], at["core"]
    near, far, twin, i1, i2 = at["near"], at["far"], at["twin"], at["i1"], at["i2"]
    greet(at)
    order = []
    for step in range((lines + 1) // 2):
        order.append(step)
        if lines - 1 - step != step:
            order.append(lines - 1 - step)

    def chip(line, j1, j2, c):
        m1 = 2 - c
        m2 = 1 + c
        return line * 4 + j1 * m1 + j2 * m2

    def f32(value):
        return value.astype(jnp.float32)

    def to_twin(line, j1, j2):
        slot = chip(line, j1, j2, 1 - core)
        return remote(
            part_ref.at[2 * slot + 1 - core], twin_in.at[slot],
            twin_send.at[slot], twin_recv.at[slot], twin,
        )

    groups = ((1 - i1, 1 - i2), (i1, 1 - i2))
    twin_groups = ((1 - i2, 1 - i1), (i2, 1 - i1), (1 - i2, i1), (i2, i1))
    for j1, j2 in twin_groups:
        for line in order:
            to_twin(line, j1, j2).start()

    def pair(line, j1, j2):
        slot = chip(line, j1, j2, core)
        remote(
            twin_in.at[slot], twin_in.at[slot], twin_send.at[slot], twin_recv.at[slot], twin
        ).wait_recv()
        return f32(part_ref[2 * slot + core]) + f32(twin_in[slot])

    def to_far(line, j1):
        slot = line * 2 + j1
        return remote(
            out_far.at[slot], far_in.at[slot], far_send.at[slot], far_recv.at[slot], far
        )

    def to_near(line):
        return remote(
            out_near.at[line], near_in.at[line], near_send.at[line], near_recv.at[line], near
        )

    def to_down(line):
        return remote(
            out_line.at[line], down_in.at[line], down_send.at[line], down_recv.at[line], me - 8
        )

    def to_up(line):
        return remote(
            out_line.at[line], up_in.at[line], up_send.at[line], up_recv.at[line], me + 8
        )

    for j1, j2 in groups:
        for line in order:
            out_far[line * 2 + j1] = pair(line, j1, j2).astype(jnp.bfloat16)
            to_far(line, j1).start()

    def after_far(line, j1):
        value = pair(line, j1, i2)
        to_far(line, j1).wait_recv()
        return value + f32(far_in[line * 2 + j1])

    for line in order:
        out_near[line] = after_far(line, 1 - i1).astype(jnp.bfloat16)
        to_near(line).start()

    def after_near(line):
        value = after_far(line, i1)
        to_near(line).wait_recv()
        return value + f32(near_in[line])

    for line in order:
        @pl.when(z > line)
        def _():
            value = after_near(line)

            @pl.when(z < lines - 1)
            def _():
                to_down(line).wait_recv()
                out_line[line] = (value + f32(down_in[line])).astype(jnp.bfloat16)

            @pl.when(z == lines - 1)
            def _():
                out_line[line] = value.astype(jnp.bfloat16)

            to_down(line).start()

        @pl.when(z < line)
        def _():
            value = after_near(line)

            @pl.when(z > 0)
            def _():
                to_up(line).wait_recv()
                out_line[line] = (value + f32(up_in[line])).astype(jnp.bfloat16)

            @pl.when(z == 0)
            def _():
                out_line[line] = value.astype(jnp.bfloat16)

            to_up(line).start()

    final = after_near(z)

    @pl.when(z == 0)
    def _():
        to_down(z).wait_recv()
        out_ref[...] = (final + f32(down_in[z])).astype(jnp.bfloat16)

    @pl.when(z == lines - 1)
    def _():
        to_up(z).wait_recv()
        out_ref[...] = (final + f32(up_in[z])).astype(jnp.bfloat16)

    @pl.when((z > 0) & (z < lines - 1))
    def _():
        to_down(z).wait_recv()
        to_up(z).wait_recv()
        out_ref[...] = (final + f32(down_in[z]) + f32(up_in[z])).astype(jnp.bfloat16)

    for line in range(lines):
        for j1 in range(2):
            to_far(line, j1).wait_send()
            for j2 in range(2):
                to_twin(line, j1, j2).wait_send()
        to_near(line).wait_send()

        @pl.when(z > line)
        def _():
            to_down(line).wait_send()

        @pl.when(z < line)
        def _():
            to_up(line).wait_send()


def gather_rows(own, n):
    return pl.pallas_call(
        functools.partial(gather_kernel, n),
        out_shape=jax.ShapeDtypeStruct((n,) + own.shape, own.dtype),
        in_specs=[pl.BlockSpec(memory_space=pltpu.VMEM)],
        out_specs=pl.BlockSpec(memory_space=pltpu.VMEM),
        scratch_shapes=[pltpu.SemaphoreType.DMA((5, n)), pltpu.SemaphoreType.DMA((n,))],
        compiler_params=pltpu.CompilerParams(
            collective_id=0, has_side_effects=True, vmem_limit_bytes=60 * 2**20
        ),
        name="gather_rows",
    )(own)


def scatter_sums(parts, n):
    block = parts.shape[1:]
    lines = n // 8

    def room(count):
        return pltpu.VMEM((count,) + block, jnp.bfloat16)

    counts = [n // 2, n // 2, 2 * lines, 2 * lines] + [lines] * 6
    return pl.pallas_call(
        functools.partial(scatter_kernel, n),
        out_shape=jax.ShapeDtypeStruct(block, jnp.bfloat16),
        in_specs=[pl.BlockSpec(memory_space=pltpu.VMEM)],
        out_specs=pl.BlockSpec(memory_space=pltpu.VMEM),
        scratch_shapes=[
            room(n // 2), room(2 * lines), room(lines), room(lines), room(lines),
            room(2 * lines), room(lines), room(lines),
        ] + [pltpu.SemaphoreType.DMA((count,)) for count in counts],
        compiler_params=pltpu.CompilerParams(
            collective_id=1, has_side_effects=True, vmem_limit_bytes=60 * 2**20
        ),
        name="scatter_sums",
    )(parts)


def dense_gates(id_block, code_block, expert_count):
    code_rows = code_block.astype(jnp.float32)
    weights = route_scale * code_rows / jnp.sum(code_rows, axis=-1, keepdims=True)
    hit = id_block[..., None] == jnp.arange(expert_count, dtype=jnp.int32)
    return jnp.sum(jnp.where(hit, weights[..., None], 0.0), axis=-2)


def shards(hidden_rows, expert_ids, gate_codes, gate_weight, up_weight, down_weight):
    n = lax.axis_size("expert")
    expert_count = n // 2
    micro_count, rows_dev, feature_count = hidden_rows.shape
    block_rows = micro_count * rows_dev
    own_expert = lax.axis_index("expert") // 2
    gates = dense_gates(expert_ids, gate_codes, expert_count).reshape(block_rows, expert_count)
    high = lax.reduce_precision(gates, 8, 7)
    width = -(-2 * expert_count // LANES) * LANES
    tail = jnp.concatenate([high, gates - high], axis=1).astype(jnp.bfloat16)
    tail = jnp.pad(tail, ((0, 0), (0, width - 2 * expert_count)))
    own = jnp.concatenate([hidden_rows.reshape(block_rows, feature_count), tail], axis=1)
    gathered = gather_rows(own, n).reshape(n * block_rows, feature_count + width)
    all_rows = gathered[:, :feature_count]
    tails = gathered[:, feature_count:].astype(jnp.float32)
    lane = jnp.arange(width, dtype=jnp.int32)
    mine = (lane == own_expert) | (lane == own_expert + expert_count)
    own_gate = jnp.sum(jnp.where(mine, tails, 0.0), axis=1, keepdims=True)
    gate_value = jnp.dot(all_rows, gate_weight, preferred_element_type=jnp.float32)
    up_value = jnp.dot(all_rows, up_weight, preferred_element_type=jnp.float32)
    hidden = (jax.nn.silu(gate_value) * up_value).astype(jnp.bfloat16)
    produced = jnp.dot(hidden, down_weight, preferred_element_type=jnp.float32)
    weighted = (produced * own_gate).astype(jnp.bfloat16)
    combined = scatter_sums(weighted.reshape(n, block_rows, feature_count), n)
    return combined.reshape(micro_count, rows_dev, feature_count)


def solution(mesh):
    return jax.shard_map(
        shards,
        mesh=mesh,
        in_specs=(
            P(None, ("groups", "expert"), None),
            P(None, ("groups", "expert"), None),
            P(None, ("groups", "expert"), None),
            P(None, "expert"),
            P(None, "expert"),
            P("expert", None),
        ),
        out_specs=P(None, ("groups", "expert"), None),
        check_vma=False,
    )
```

```python
import functools
import math

import jax
import jax.numpy as jnp
from jax import lax
from jax.experimental import pallas as pl
from jax.experimental.pallas import tpu as pltpu
from jax.sharding import PartitionSpec as P

route_scale = 2.5
LANES = 128


def place(n):
    me = lax.axis_index("expert")
    core, x, y, z = me % 2, (me // 2) % 2, (me // 4) % 2, me // 8
    to_y, to_x = me + 4 - 8 * y, me + 2 - 4 * x
    return dict(
        me=me, core=core, z=z, lines=n // 8,
        near=to_y * (1 - core) + to_x * core,
        far=to_x * (1 - core) + to_y * core,
        twin=me + 1 - 2 * core,
        i1=y * (1 - core) + x * core,
        i2=x * (1 - core) + y * core,
    )


def greet(at):
    barrier = pltpu.get_barrier_semaphore()
    z, lines = at["z"], at["lines"]

    def signal(device):
        pl.semaphore_signal(
            barrier, inc=1, device_id={"expert": device},
            device_id_type=pl.DeviceIdType.MESH,
        )

    for name in ("near", "far", "twin"):
        signal(at[name])

    @pl.when(z > 0)
    def _():
        signal(at["me"] - 8)

    @pl.when(z < lines - 1)
    def _():
        signal(at["me"] + 8)

    on_line = (z + lines - 1) // lines + (2 * lines - 2 - z) // lines
    pl.semaphore_wait(barrier, 3 + on_line)


def remote(src, dst, send_sem, recv_sem, device):
    return pltpu.make_async_remote_copy(
        src_ref=src, dst_ref=dst, send_sem=send_sem, recv_sem=recv_sem,
        device_id={"expert": device}, device_id_type=pl.DeviceIdType.MESH,
    )


def gather_kernel(n, own_ref, out_ref, send_sem, recv_sem, work=None, between=None):
    at = place(n)
    me, z, lines = at["me"], at["z"], at["lines"]
    near, far, twin = at["near"], at["far"], at["twin"]
    both = near + far - me
    greet(at)

    def send(kind, source, device, begin, first=False):
        copy = remote(
            own_ref if first else out_ref.at[source], out_ref.at[source],
            send_sem.at[kind, source], recv_sem.at[source], device,
        )
        if begin:
            copy.start()
        else:
            copy.wait_send()

    def arrived(source):
        remote(
            out_ref.at[source], out_ref.at[source],
            send_sem.at[0, source], recv_sem.at[source], twin,
        ).wait_recv()

    def line_sends(source, begin, up, down, first=False):
        if up:
            @pl.when(z < lines - 1)
            def _():
                send(0, source, me + 8, begin, first)
        if down:
            @pl.when(z > 0)
            def _():
                send(1, source, me - 8, begin, first)
        send(2, source, near, begin, first)
        send(3, source, far, begin, first)
        send(4, source, twin, begin, first)

    def line_step(k, begin):
        @pl.when(z >= k)
        def _():
            if begin:
                arrived(me - 8 * k)
            line_sends(me - 8 * k, begin, True, False)

        @pl.when(z + k < lines)
        def _():
            if begin:
                arrived(me + 8 * k)
            line_sends(me + 8 * k, begin, False, True)

    def side_step(base, k, to_far, begin):
        def one(source):
            if begin:
                arrived(source)
            if to_far:
                send(3, source, far, begin)
            send(4, source, twin, begin)

        if k == 0:
            one(base)
            return

        @pl.when(z >= k)
        def _():
            one(base - 8 * k)

        @pl.when(z + k < lines)
        def _():
            one(base + 8 * k)

    line_sends(me, True, True, True, True)
    out_ref[me] = own_ref[...]
    def twins_arrived(group):
        for line in range(lines):
            arrived(group + 8 * line + 1 - at["core"])

    def work_on(device):
        group = device - at["core"] - 8 * z
        twins_arrived(group)
        if work is not None:
            work(group)

    for k in range(1, lines + 1):
        if k < lines:
            line_step(k, True)
        side_step(near, k - 1, True, True)
    work_on(me)
    for k in range(lines):
        side_step(far, k, False, True)
    work_on(near)
    for k in range(lines):
        side_step(both, k, False, True)
    work_on(far)
    if between is not None:
        between()
    work_on(both)
    line_sends(me, False, True, True, True)
    for k in range(lines):
        if k > 0:
            line_step(k, False)
        side_step(near, k, True, False)
        side_step(far, k, False, False)
        side_step(both, k, False, False)


def scatter_kernel(
    n, part_ref, *refs
):
    at = place(n)
    greet(at)
    start_twins, far_sends, finish = scatter_pieces(n, part_ref, *refs)
    near, far, me = at["near"], at["far"], at["me"]
    for device in (near + far - me, far, near, me):
        start_twins(device - at["core"] - 8 * at["z"])
    far_sends(False)
    far_sends(True)
    finish()


def scatter_pieces(
    n, part_ref, out_ref, twin_in, far_in, near_in, down_in, up_in, out_far, out_near, out_line,
    twin_send, twin_recv, far_send, far_recv, near_send, near_recv,
    down_send, down_recv, up_send, up_recv,
):
    at = place(n)
    me, z, lines, core = at["me"], at["z"], at["lines"], at["core"]
    near, far, twin, i1, i2 = at["near"], at["far"], at["twin"], at["i1"], at["i2"]
    order = []
    for step in range((lines + 1) // 2):
        order.append(step)
        if lines - 1 - step != step:
            order.append(lines - 1 - step)

    def chip(line, j1, j2, c):
        m1 = 2 - c
        m2 = 1 + c
        return line * 4 + j1 * m1 + j2 * m2

    def f32(value):
        return value.astype(jnp.float32)

    def to_twin(slot):
        return remote(
            part_ref.at[2 * slot + 1 - core], twin_in.at[slot],
            twin_send.at[slot], twin_recv.at[slot], twin,
        )

    def start_twins(group):
        for line in order:
            to_twin(group // 2 + 4 * line).start()

    def pair(line, j1, j2):
        slot = chip(line, j1, j2, core)
        remote(
            twin_in.at[slot], twin_in.at[slot], twin_send.at[slot], twin_recv.at[slot], twin
        ).wait_recv()
        return f32(part_ref[2 * slot + core]) + f32(twin_in[slot])

    def to_far(line, j1):
        slot = line * 2 + j1
        return remote(
            out_far.at[slot], far_in.at[slot], far_send.at[slot], far_recv.at[slot], far
        )

    def to_near(line):
        return remote(
            out_near.at[line], near_in.at[line], near_send.at[line], near_recv.at[line], near
        )

    def to_down(line):
        return remote(
            out_line.at[line], down_in.at[line], down_send.at[line], down_recv.at[line], me - 8
        )

    def to_up(line):
        return remote(
            out_line.at[line], up_in.at[line], up_send.at[line], up_recv.at[line], me + 8
        )

    def far_sends(both):
        j1 = 1 - i1 if both else i1
        for line in order:
            out_far[line * 2 + j1] = pair(line, j1, 1 - i2).astype(jnp.bfloat16)
            to_far(line, j1).start()

    def after_far(line, j1):
        value = pair(line, j1, i2)
        to_far(line, j1).wait_recv()
        return value + f32(far_in[line * 2 + j1])

    def finish():
        for line in order:
            out_near[line] = after_far(line, 1 - i1).astype(jnp.bfloat16)
            to_near(line).start()

        def after_near(line):
            value = after_far(line, i1)
            to_near(line).wait_recv()
            return value + f32(near_in[line])

        for line in order:
            @pl.when(z > line)
            def _():
                value = after_near(line)

                @pl.when(z < lines - 1)
                def _():
                    to_down(line).wait_recv()
                    out_line[line] = (value + f32(down_in[line])).astype(jnp.bfloat16)

                @pl.when(z == lines - 1)
                def _():
                    out_line[line] = value.astype(jnp.bfloat16)

                to_down(line).start()

            @pl.when(z < line)
            def _():
                value = after_near(line)

                @pl.when(z > 0)
                def _():
                    to_up(line).wait_recv()
                    out_line[line] = (value + f32(up_in[line])).astype(jnp.bfloat16)

                @pl.when(z == 0)
                def _():
                    out_line[line] = value.astype(jnp.bfloat16)

                to_up(line).start()

        final = after_near(z)

        @pl.when(z == 0)
        def _():
            to_down(z).wait_recv()
            out_ref[...] = (final + f32(down_in[z])).astype(jnp.bfloat16)

        @pl.when(z == lines - 1)
        def _():
            to_up(z).wait_recv()
            out_ref[...] = (final + f32(up_in[z])).astype(jnp.bfloat16)

        @pl.when((z > 0) & (z < lines - 1))
        def _():
            to_down(z).wait_recv()
            to_up(z).wait_recv()
            out_ref[...] = (final + f32(down_in[z]) + f32(up_in[z])).astype(jnp.bfloat16)

        for line in range(lines):
            for j1 in range(2):
                to_far(line, j1).wait_send()
                for j2 in range(2):
                    to_twin(4 * line + 2 * j1 + j2).wait_send()
            to_near(line).wait_send()

            @pl.when(z > line)
            def _():
                to_down(line).wait_send()

            @pl.when(z < line)
            def _():
                to_up(line).wait_send()

    return start_twins, far_sends, finish


def fused_kernel(
    n, own_ref, gate_hbm, up_hbm, down_hbm, out_ref,
    all_ref, part_ref, gate_ref, up_ref, down_ref, left_ref, act_ref, scale_ref,
    load_sem, send_sem, recv_sem, *refs
):
    at = place(n)
    lines = n // 8
    rows, features = part_ref.shape[1:]
    hidden = act_ref.shape[1]
    loads = [
        pltpu.make_async_copy(source, target, load_sem.at[i])
        for i, (source, target) in enumerate(
            ((gate_hbm, gate_ref), (up_hbm, up_ref), (down_hbm, down_ref))
        )
    ]
    for load in loads:
        load.start()
    start_twins, far_sends, finish = scatter_pieces(n, part_ref, out_ref, *refs)
    loaded = []

    def work(group):
        if not loaded:
            for load in loads:
                load.wait()
            loaded.append(True)
        width = all_ref.shape[2] - features
        lane = lax.broadcasted_iota(jnp.int32, (rows, width), 1)
        own_expert = at["me"] // 2
        mine = (lane == own_expert) | (lane == own_expert + n // 2)
        for line in range(lines):
            for core in range(2):
                index = group + 8 * line + core
                base = (2 * line + core) * rows
                left_ref[base:base + rows, :] = all_ref[index, :, :features]
                tail = all_ref[index, :, features:].astype(jnp.float32)
                scale = jnp.sum(jnp.where(mine, tail, 0.0), axis=1, keepdims=True)
                scale_ref[base:base + rows, :] = jnp.broadcast_to(scale, (rows, LANES))
        step = min(hidden, 2 * LANES)

        @pl.loop(0, hidden // step)
        def _(tile):
            columns = pl.ds(pl.multiple_of(tile * step, step), step)
            gate = jnp.dot(
                left_ref[...], gate_ref[:, columns], preferred_element_type=jnp.float32
            )
            up = jnp.dot(left_ref[...], up_ref[:, columns], preferred_element_type=jnp.float32)
            act_ref[:, columns] = (gate / (1.0 + jnp.exp(-gate)) * up).astype(jnp.bfloat16)

        wide = min(features, 4 * LANES)

        @pl.loop(0, features // wide)
        def _(tile):
            columns = pl.ds(pl.multiple_of(tile * wide, wide), wide)
            part = jnp.dot(
                act_ref[...], down_ref[:, columns], preferred_element_type=jnp.float32
            )
            part = (part * scale_ref[:, :1]).astype(jnp.bfloat16)
            for line in range(lines):
                for core in range(2):
                    base = (2 * line + core) * rows
                    part_ref[group + 8 * line + core, :, columns] = part[base:base + rows, :]

        start_twins(group)

    gather_kernel(
        n, own_ref, all_ref, send_sem, recv_sem, work, lambda: far_sends(False)
    )
    far_sends(True)
    finish()


def fused(own, gate_weight, up_weight, down_weight, n):
    rows = own.shape[0]
    hidden, features = down_weight.shape
    lines = n // 8
    block = (rows, features)

    def room(*shape):
        return pltpu.VMEM(shape, jnp.bfloat16)

    arrays = [
        (n,) + own.shape, (n,) + block, gate_weight.shape, up_weight.shape, down_weight.shape,
        (lines * 2 * rows, features), (lines * 2 * rows, hidden),
    ]
    slots = [
        (count,) + block
        for count in (n // 2, 2 * lines, lines, lines, lines, 2 * lines, lines, lines)
    ]
    counts = [n // 2, n // 2, 2 * lines, 2 * lines] + [lines] * 6
    if sum(2 * math.prod(shape) for shape in arrays + slots) > 52 * 2**20:
        return None
    anywhere = pl.BlockSpec(memory_space=pl.ANY)
    return pl.pallas_call(
        functools.partial(fused_kernel, n),
        out_shape=jax.ShapeDtypeStruct(block, jnp.bfloat16),
        in_specs=[pl.BlockSpec(memory_space=pltpu.VMEM), anywhere, anywhere, anywhere],
        out_specs=pl.BlockSpec(memory_space=pltpu.VMEM),
        scratch_shapes=[room(*shape) for shape in arrays] + [
            pltpu.VMEM((lines * 2 * rows, LANES), jnp.float32),
            pltpu.SemaphoreType.DMA((3,)),
            pltpu.SemaphoreType.DMA((5, n)), pltpu.SemaphoreType.DMA((n,)),
        ] + [room(*shape) for shape in slots]
        + [pltpu.SemaphoreType.DMA((count,)) for count in counts],
        compiler_params=pltpu.CompilerParams(
            collective_id=2, has_side_effects=True, vmem_limit_bytes=60 * 2**20
        ),
        name="fused",
    )(own, gate_weight, up_weight, down_weight)


def gather_rows(own, n):
    return pl.pallas_call(
        functools.partial(gather_kernel, n),
        out_shape=jax.ShapeDtypeStruct((n,) + own.shape, own.dtype),
        in_specs=[pl.BlockSpec(memory_space=pltpu.VMEM)],
        out_specs=pl.BlockSpec(memory_space=pltpu.VMEM),
        scratch_shapes=[pltpu.SemaphoreType.DMA((5, n)), pltpu.SemaphoreType.DMA((n,))],
        compiler_params=pltpu.CompilerParams(
            collective_id=0, has_side_effects=True, vmem_limit_bytes=60 * 2**20
        ),
        name="gather_rows",
    )(own)


def scatter_sums(parts, n):
    block = parts.shape[1:]
    lines = n // 8

    def room(count):
        return pltpu.VMEM((count,) + block, jnp.bfloat16)

    counts = [n // 2, n // 2, 2 * lines, 2 * lines] + [lines] * 6
    return pl.pallas_call(
        functools.partial(scatter_kernel, n),
        out_shape=jax.ShapeDtypeStruct(block, jnp.bfloat16),
        in_specs=[pl.BlockSpec(memory_space=pltpu.VMEM)],
        out_specs=pl.BlockSpec(memory_space=pltpu.VMEM),
        scratch_shapes=[
            room(n // 2), room(2 * lines), room(lines), room(lines), room(lines),
            room(2 * lines), room(lines), room(lines),
        ] + [pltpu.SemaphoreType.DMA((count,)) for count in counts],
        compiler_params=pltpu.CompilerParams(
            collective_id=1, has_side_effects=True, vmem_limit_bytes=60 * 2**20
        ),
        name="scatter_sums",
    )(parts)


def dense_gates(id_block, code_block, expert_count):
    code_rows = code_block.astype(jnp.float32)
    weights = route_scale * code_rows / jnp.sum(code_rows, axis=-1, keepdims=True)
    hit = id_block[..., None] == jnp.arange(expert_count, dtype=jnp.int32)
    return jnp.sum(jnp.where(hit, weights[..., None], 0.0), axis=-2)


def shards(hidden_rows, expert_ids, gate_codes, gate_weight, up_weight, down_weight):
    n = lax.axis_size("expert")
    expert_count = n // 2
    micro_count, rows_dev, feature_count = hidden_rows.shape
    block_rows = micro_count * rows_dev
    own_expert = lax.axis_index("expert") // 2
    gates = dense_gates(expert_ids, gate_codes, expert_count).reshape(block_rows, expert_count)
    high = lax.reduce_precision(gates, 8, 7)
    width = -(-2 * expert_count // LANES) * LANES
    tail = jnp.concatenate([high, gates - high], axis=1).astype(jnp.bfloat16)
    tail = jnp.pad(tail, ((0, 0), (0, width - 2 * expert_count)))
    own = jnp.concatenate([hidden_rows.reshape(block_rows, feature_count), tail], axis=1)
    combined = fused(own, gate_weight, up_weight, down_weight, n)
    if combined is not None:
        return combined.reshape(micro_count, rows_dev, feature_count)
    gathered = gather_rows(own, n).reshape(n * block_rows, feature_count + width)
    all_rows = gathered[:, :feature_count]
    tails = gathered[:, feature_count:].astype(jnp.float32)
    lane = jnp.arange(width, dtype=jnp.int32)
    mine = (lane == own_expert) | (lane == own_expert + expert_count)
    own_gate = jnp.sum(jnp.where(mine, tails, 0.0), axis=1, keepdims=True)
    gate_value = jnp.dot(all_rows, gate_weight, preferred_element_type=jnp.float32)
    up_value = jnp.dot(all_rows, up_weight, preferred_element_type=jnp.float32)
    hidden = (jax.nn.silu(gate_value) * up_value).astype(jnp.bfloat16)
    produced = jnp.dot(hidden, down_weight, preferred_element_type=jnp.float32)
    weighted = (produced * own_gate).astype(jnp.bfloat16)
    combined = scatter_sums(weighted.reshape(n, block_rows, feature_count), n)
    return combined.reshape(micro_count, rows_dev, feature_count)


def solution(mesh):
    return jax.shard_map(
        shards,
        mesh=mesh,
        in_specs=(
            P(None, ("groups", "expert"), None),
            P(None, ("groups", "expert"), None),
            P(None, ("groups", "expert"), None),
            P(None, "expert"),
            P(None, "expert"),
            P("expert", None),
        ),
        out_specs=P(None, ("groups", "expert"), None),
        check_vma=False,
    )
```

```python
import functools
import math

import jax
import jax.numpy as jnp
from jax import lax
from jax.experimental import pallas as pl
from jax.experimental.pallas import tpu as pltpu
from jax.sharding import PartitionSpec as P

route_scale = 2.5
LANES = 128
PIECES = 2


def span(piece, size):
    step = size // PIECES // LANES * LANES
    return slice(piece * step, size if piece == PIECES - 1 else (piece + 1) * step)


def place(n):
    me = lax.axis_index("expert")
    core, x, y, z = me % 2, (me // 2) % 2, (me // 4) % 2, me // 8
    to_y, to_x = me + 4 - 8 * y, me + 2 - 4 * x
    return dict(
        me=me, core=core, z=z, lines=n // 8,
        near=to_y * (1 - core) + to_x * core,
        far=to_x * (1 - core) + to_y * core,
        twin=me + 1 - 2 * core,
        i1=y * (1 - core) + x * core,
        i2=x * (1 - core) + y * core,
    )


def greet(at):
    barrier = pltpu.get_barrier_semaphore()
    z, lines = at["z"], at["lines"]

    def signal(device):
        pl.semaphore_signal(
            barrier, inc=1, device_id={"expert": device},
            device_id_type=pl.DeviceIdType.MESH,
        )

    for name in ("near", "far", "twin"):
        signal(at[name])

    @pl.when(z > 0)
    def _():
        signal(at["me"] - 8)

    @pl.when(z < lines - 1)
    def _():
        signal(at["me"] + 8)

    on_line = (z + lines - 1) // lines + (2 * lines - 2 - z) // lines
    pl.semaphore_wait(barrier, 3 + on_line)


def remote(src, dst, send_sem, recv_sem, device):
    return pltpu.make_async_remote_copy(
        src_ref=src, dst_ref=dst, send_sem=send_sem, recv_sem=recv_sem,
        device_id={"expert": device}, device_id_type=pl.DeviceIdType.MESH,
    )


def gather_kernel(n, own_ref, out_ref, send_sem, recv_sem, work=None, between=None):
    at = place(n)
    me, z, lines = at["me"], at["z"], at["lines"]
    near, far, twin = at["near"], at["far"], at["twin"]
    both = near + far - me
    greet(at)

    def send(kind, source, piece, device, begin, first=False):
        columns = span(piece, own_ref.shape[1])
        here = out_ref.at[source, :, columns]
        copy = remote(
            own_ref.at[:, columns] if first else here, here,
            send_sem.at[kind, source * PIECES + piece],
            recv_sem.at[source * PIECES + piece], device,
        )
        if begin:
            copy.start()
        else:
            copy.wait_send()

    def arrived_piece(source, piece):
        here = out_ref.at[source, :, span(piece, own_ref.shape[1])]
        remote(
            here, here, send_sem.at[0, source * PIECES + piece],
            recv_sem.at[source * PIECES + piece], twin,
        ).wait_recv()

    def arrived(source):
        for piece in range(PIECES):
            arrived_piece(source, piece)

    def line_sends(source, begin, up, down, first=False):
        for piece in range(PIECES):
            if begin and not first:
                arrived_piece(source, piece)
            if up:
                @pl.when(z < lines - 1)
                def _():
                    send(0, source, piece, me + 8, begin, first)
            if down:
                @pl.when(z > 0)
                def _():
                    send(1, source, piece, me - 8, begin, first)
            send(2, source, piece, near, begin, first)
            send(3, source, piece, far, begin, first)
            send(4, source, piece, twin, begin, first)

    def line_step(k, begin):
        @pl.when(z >= k)
        def _():
            line_sends(me - 8 * k, begin, True, False)

        @pl.when(z + k < lines)
        def _():
            line_sends(me + 8 * k, begin, False, True)

    def side_step(base, k, to_far, begin):
        def one(source):
            for piece in range(PIECES):
                if begin:
                    arrived_piece(source, piece)
                if to_far:
                    send(3, source, piece, far, begin)
                send(4, source, piece, twin, begin)

        if k == 0:
            one(base)
            return

        @pl.when(z >= k)
        def _():
            one(base - 8 * k)

        @pl.when(z + k < lines)
        def _():
            one(base + 8 * k)

    line_sends(me, True, True, True, True)
    out_ref[me] = own_ref[...]
    def twins_arrived(group):
        for line in range(lines):
            arrived(group + 8 * line + 1 - at["core"])

    def work_on(*devices):
        groups = [device - at["core"] - 8 * z for device in devices]
        for group in groups:
            twins_arrived(group)
        if work is not None:
            work(groups)

    for k in range(1, lines + 1):
        if k < lines:
            line_step(k, True)
        side_step(near, k - 1, True, True)
    for k in range(lines):
        side_step(far, k, False, True)
    work_on(me, near, far)
    for k in range(lines):
        side_step(both, k, False, True)
    if between is not None:
        between()
    work_on(both)
    line_sends(me, False, True, True, True)
    for k in range(lines):
        if k > 0:
            line_step(k, False)
        side_step(near, k, True, False)
        side_step(far, k, False, False)
        side_step(both, k, False, False)


def scatter_kernel(
    n, part_ref, *refs
):
    at = place(n)
    greet(at)
    start_twins, far_sends, finish = scatter_pieces(n, part_ref, *refs)
    near, far, me = at["near"], at["far"], at["me"]
    for device in (near + far - me, far, near, me):
        start_twins(device - at["core"] - 8 * at["z"])
    far_sends(False)
    far_sends(True)
    finish()


def scatter_pieces(
    n, part_ref, out_ref, twin_in, far_in, near_in, down_in, up_in, out_far, out_near, out_line,
    twin_send, twin_recv, far_send, far_recv, near_send, near_recv,
    down_send, down_recv, up_send, up_recv,
):
    at = place(n)
    me, z, lines, core = at["me"], at["z"], at["lines"], at["core"]
    near, far, twin, i1, i2 = at["near"], at["far"], at["twin"], at["i1"], at["i2"]
    order = []
    for step in range((lines + 1) // 2):
        order.append(step)
        if lines - 1 - step != step:
            order.append(lines - 1 - step)

    def chip(line, j1, j2, c):
        m1 = 2 - c
        m2 = 1 + c
        return line * 4 + j1 * m1 + j2 * m2

    def f32(value):
        return value.astype(jnp.float32)

    def moved(source, target, sems, slot, piece, device):
        columns = span(piece, part_ref.shape[2])
        send_sem, recv_sem = sems
        at_sem = slot * PIECES + piece
        return remote(
            source.at[:, columns], target.at[slot, :, columns],
            send_sem.at[at_sem], recv_sem.at[at_sem], device,
        )

    pieces = range(PIECES)

    def to_twin(slot, piece):
        source = part_ref.at[2 * slot + 1 - core]
        return moved(source, twin_in, (twin_send, twin_recv), slot, piece, twin)

    def start_twins(group):
        for line in order:
            for piece in pieces:
                to_twin(group // 2 + 4 * line, piece).start()

    def pair(line, j1, j2, piece):
        columns = span(piece, part_ref.shape[2])
        slot = chip(line, j1, j2, core)
        moved(
            twin_in.at[slot], twin_in, (twin_send, twin_recv), slot, piece, twin
        ).wait_recv()
        return f32(part_ref[2 * slot + core, :, columns]) + f32(twin_in[slot, :, columns])

    def to_far(line, j1, piece):
        slot = line * 2 + j1
        return moved(out_far.at[slot], far_in, (far_send, far_recv), slot, piece, far)

    def to_near(line, piece):
        return moved(out_near.at[line], near_in, (near_send, near_recv), line, piece, near)

    def to_down(line, piece):
        return moved(out_line.at[line], down_in, (down_send, down_recv), line, piece, me - 8)

    def to_up(line, piece):
        return moved(out_line.at[line], up_in, (up_send, up_recv), line, piece, me + 8)

    def far_sends(both):
        j1 = 1 - i1 if both else i1
        for line in order:
            for piece in pieces:
                columns = span(piece, part_ref.shape[2])
                value = pair(line, j1, 1 - i2, piece)
                out_far[line * 2 + j1, :, columns] = value.astype(jnp.bfloat16)
                to_far(line, j1, piece).start()

    def after_far(line, j1, piece):
        value = pair(line, j1, i2, piece)
        to_far(line, j1, piece).wait_recv()
        return value + f32(far_in[line * 2 + j1, :, span(piece, part_ref.shape[2])])

    def after_near(line, piece):
        value = after_far(line, i1, piece)
        to_near(line, piece).wait_recv()
        return value + f32(near_in[line, :, span(piece, part_ref.shape[2])])

    def line_sends(line, piece, begin):
        columns = span(piece, part_ref.shape[2])

        def one(copy, edge, landed):
            value = after_near(line, piece)

            @pl.when(edge)
            def _():
                out_line[line, :, columns] = value.astype(jnp.bfloat16)

            @pl.when(jnp.logical_not(edge))
            def _():
                copy.wait_recv()
                total = value + f32(landed[line, :, columns])
                out_line[line, :, columns] = total.astype(jnp.bfloat16)

            copy.start()

        @pl.when(z > line)
        def _():
            if begin:
                one(to_down(line, piece), z == lines - 1, down_in)
            else:
                to_down(line, piece).wait_send()

        @pl.when(z < line)
        def _():
            if begin:
                one(to_up(line, piece), z == 0, up_in)
            else:
                to_up(line, piece).wait_send()

    def finish():
        for line in order:
            for piece in pieces:
                columns = span(piece, part_ref.shape[2])
                value = after_far(line, 1 - i1, piece)
                out_near[line, :, columns] = value.astype(jnp.bfloat16)
                to_near(line, piece).start()
        for line in order:
            for piece in pieces:
                line_sends(line, piece, True)
        for piece in pieces:
            columns = span(piece, part_ref.shape[2])
            final = after_near(z, piece)

            @pl.when(z == 0)
            def _():
                to_down(z, piece).wait_recv()
                out_ref[:, columns] = (final + f32(down_in[z, :, columns])).astype(jnp.bfloat16)

            @pl.when(z == lines - 1)
            def _():
                to_up(z, piece).wait_recv()
                out_ref[:, columns] = (final + f32(up_in[z, :, columns])).astype(jnp.bfloat16)

            @pl.when((z > 0) & (z < lines - 1))
            def _():
                to_down(z, piece).wait_recv()
                to_up(z, piece).wait_recv()
                total = final + f32(down_in[z, :, columns]) + f32(up_in[z, :, columns])
                out_ref[:, columns] = total.astype(jnp.bfloat16)

        for line in range(lines):
            for piece in pieces:
                for j1 in range(2):
                    to_far(line, j1, piece).wait_send()
                    for j2 in range(2):
                        to_twin(4 * line + 2 * j1 + j2, piece).wait_send()
                to_near(line, piece).wait_send()
                line_sends(line, piece, False)

    return start_twins, far_sends, finish


def fused_kernel(
    n, own_ref, gate_hbm, up_hbm, down_hbm, out_ref,
    all_ref, part_ref, gate_ref, up_ref, down_ref, left_ref, act_ref, scale_ref,
    load_sem, send_sem, recv_sem, *refs
):
    at = place(n)
    lines = n // 8
    rows, features = part_ref.shape[1:]
    hidden = act_ref.shape[1]
    loads = [
        pltpu.make_async_copy(source, target, load_sem.at[i])
        for i, (source, target) in enumerate(
            ((gate_hbm, gate_ref), (up_hbm, up_ref), (down_hbm, down_ref))
        )
    ]
    for load in loads:
        load.start()
    start_twins, far_sends, finish = scatter_pieces(n, part_ref, out_ref, *refs)
    loaded = []

    def work(groups):
        if not loaded:
            for load in loads:
                load.wait()
            loaded.append(True)
        width = all_ref.shape[2] - features
        lane = lax.broadcasted_iota(jnp.int32, (rows, width), 1)
        own_expert = at["me"] // 2
        mine = (lane == own_expert) | (lane == own_expert + n // 2)
        places = [
            (group + 8 * line + core, ((order * lines + line) * 2 + core) * rows)
            for order, group in enumerate(groups) for line in range(lines) for core in range(2)
        ]
        total = len(places) * rows
        for index, base in places:
            left_ref[base:base + rows, :] = all_ref[index, :, :features]
            tail = all_ref[index, :, features:].astype(jnp.float32)
            scale = jnp.sum(jnp.where(mine, tail, 0.0), axis=1, keepdims=True)
            scale_ref[base:base + rows, :] = jnp.broadcast_to(scale, (rows, LANES))
        step = min(hidden, 2 * LANES)

        @pl.loop(0, hidden // step)
        def _(tile):
            columns = pl.ds(pl.multiple_of(tile * step, step), step)
            gate = jnp.dot(
                left_ref[:total, :], gate_ref[:, columns], preferred_element_type=jnp.float32
            )
            up = jnp.dot(
                left_ref[:total, :], up_ref[:, columns], preferred_element_type=jnp.float32
            )
            act_ref[:total, columns] = (gate / (1.0 + jnp.exp(-gate)) * up).astype(jnp.bfloat16)

        wide = min(features, 4 * LANES)

        @pl.loop(0, features // wide)
        def _(tile):
            columns = pl.ds(pl.multiple_of(tile * wide, wide), wide)
            part = jnp.dot(
                act_ref[:total, :], down_ref[:, columns], preferred_element_type=jnp.float32
            )
            part = (part * scale_ref[:total, :1]).astype(jnp.bfloat16)
            for index, base in places:
                part_ref[index, :, columns] = part[base:base + rows, :]

        for group in groups:
            start_twins(group)

    gather_kernel(
        n, own_ref, all_ref, send_sem, recv_sem, work, lambda: far_sends(False)
    )
    far_sends(True)
    finish()


def fused(own, gate_weight, up_weight, down_weight, n):
    rows = own.shape[0]
    hidden, features = down_weight.shape
    lines = n // 8
    block = (rows, features)

    def room(*shape):
        return pltpu.VMEM(shape, jnp.bfloat16)

    arrays = [
        (n,) + own.shape, (n,) + block, gate_weight.shape, up_weight.shape, down_weight.shape,
        (lines * 6 * rows, features), (lines * 6 * rows, hidden),
    ]
    slots = [
        (count,) + block
        for count in (n // 2, 2 * lines, lines, lines, lines, 2 * lines, lines, lines)
    ]
    counts = [n // 2, n // 2, 2 * lines, 2 * lines] + [lines] * 6
    if sum(2 * math.prod(shape) for shape in arrays + slots) > 52 * 2**20:
        return None
    anywhere = pl.BlockSpec(memory_space=pl.ANY)
    return pl.pallas_call(
        functools.partial(fused_kernel, n),
        out_shape=jax.ShapeDtypeStruct(block, jnp.bfloat16),
        in_specs=[pl.BlockSpec(memory_space=pltpu.VMEM), anywhere, anywhere, anywhere],
        out_specs=pl.BlockSpec(memory_space=pltpu.VMEM),
        scratch_shapes=[room(*shape) for shape in arrays] + [
            pltpu.VMEM((lines * 6 * rows, LANES), jnp.float32),
            pltpu.SemaphoreType.DMA((3,)),
            pltpu.SemaphoreType.DMA((5, n * PIECES)), pltpu.SemaphoreType.DMA((n * PIECES,)),
        ] + [room(*shape) for shape in slots]
        + [pltpu.SemaphoreType.DMA((count * PIECES,)) for count in counts],
        compiler_params=pltpu.CompilerParams(
            collective_id=2, has_side_effects=True, vmem_limit_bytes=60 * 2**20
        ),
        name="fused",
    )(own, gate_weight, up_weight, down_weight)


def gather_rows(own, n):
    return pl.pallas_call(
        functools.partial(gather_kernel, n),
        out_shape=jax.ShapeDtypeStruct((n,) + own.shape, own.dtype),
        in_specs=[pl.BlockSpec(memory_space=pltpu.VMEM)],
        out_specs=pl.BlockSpec(memory_space=pltpu.VMEM),
        scratch_shapes=[pltpu.SemaphoreType.DMA((5, n * PIECES)), pltpu.SemaphoreType.DMA((n * PIECES,))],
        compiler_params=pltpu.CompilerParams(
            collective_id=0, has_side_effects=True, vmem_limit_bytes=60 * 2**20
        ),
        name="gather_rows",
    )(own)


def scatter_sums(parts, n):
    block = parts.shape[1:]
    lines = n // 8

    def room(count):
        return pltpu.VMEM((count,) + block, jnp.bfloat16)

    counts = [n // 2, n // 2, 2 * lines, 2 * lines] + [lines] * 6
    return pl.pallas_call(
        functools.partial(scatter_kernel, n),
        out_shape=jax.ShapeDtypeStruct(block, jnp.bfloat16),
        in_specs=[pl.BlockSpec(memory_space=pltpu.VMEM)],
        out_specs=pl.BlockSpec(memory_space=pltpu.VMEM),
        scratch_shapes=[
            room(n // 2), room(2 * lines), room(lines), room(lines), room(lines),
            room(2 * lines), room(lines), room(lines),
        ] + [pltpu.SemaphoreType.DMA((count * PIECES,)) for count in counts],
        compiler_params=pltpu.CompilerParams(
            collective_id=1, has_side_effects=True, vmem_limit_bytes=60 * 2**20
        ),
        name="scatter_sums",
    )(parts)


def dense_gates(id_block, code_block, expert_count):
    code_rows = code_block.astype(jnp.float32)
    weights = route_scale * code_rows / jnp.sum(code_rows, axis=-1, keepdims=True)
    hit = id_block[..., None] == jnp.arange(expert_count, dtype=jnp.int32)
    return jnp.sum(jnp.where(hit, weights[..., None], 0.0), axis=-2)


def shards(hidden_rows, expert_ids, gate_codes, gate_weight, up_weight, down_weight):
    n = lax.axis_size("expert")
    expert_count = n // 2
    micro_count, rows_dev, feature_count = hidden_rows.shape
    block_rows = micro_count * rows_dev
    own_expert = lax.axis_index("expert") // 2
    gates = dense_gates(expert_ids, gate_codes, expert_count).reshape(block_rows, expert_count)
    high = lax.reduce_precision(gates, 8, 7)
    width = -(-2 * expert_count // LANES) * LANES
    tail = jnp.concatenate([high, gates - high], axis=1).astype(jnp.bfloat16)
    tail = jnp.pad(tail, ((0, 0), (0, width - 2 * expert_count)))
    own = jnp.concatenate([hidden_rows.reshape(block_rows, feature_count), tail], axis=1)
    combined = fused(own, gate_weight, up_weight, down_weight, n)
    if combined is not None:
        return combined.reshape(micro_count, rows_dev, feature_count)
    gathered = gather_rows(own, n).reshape(n * block_rows, feature_count + width)
    all_rows = gathered[:, :feature_count]
    tails = gathered[:, feature_count:].astype(jnp.float32)
    lane = jnp.arange(width, dtype=jnp.int32)
    mine = (lane == own_expert) | (lane == own_expert + expert_count)
    own_gate = jnp.sum(jnp.where(mine, tails, 0.0), axis=1, keepdims=True)
    gate_value = jnp.dot(all_rows, gate_weight, preferred_element_type=jnp.float32)
    up_value = jnp.dot(all_rows, up_weight, preferred_element_type=jnp.float32)
    hidden = (jax.nn.silu(gate_value) * up_value).astype(jnp.bfloat16)
    produced = jnp.dot(hidden, down_weight, preferred_element_type=jnp.float32)
    weighted = (produced * own_gate).astype(jnp.bfloat16)
    combined = scatter_sums(weighted.reshape(n, block_rows, feature_count), n)
    return combined.reshape(micro_count, rows_dev, feature_count)


def solution(mesh):
    return jax.shard_map(
        shards,
        mesh=mesh,
        in_specs=(
            P(None, ("groups", "expert"), None),
            P(None, ("groups", "expert"), None),
            P(None, ("groups", "expert"), None),
            P(None, "expert"),
            P(None, "expert"),
            P("expert", None),
        ),
        out_specs=P(None, ("groups", "expert"), None),
        check_vma=False,
    )
```

```python
import functools
import math

import jax
import jax.numpy as jnp
from jax import lax
from jax.experimental import pallas as pl
from jax.experimental.pallas import tpu as pltpu
from jax.sharding import PartitionSpec as P

route_scale = 2.5
LANES = 128
PIECES = 1


def span(piece, size):
    step = size // PIECES // LANES * LANES
    return slice(piece * step, size if piece == PIECES - 1 else (piece + 1) * step)


def place(n):
    me = lax.axis_index("expert")
    core, x, y, z = me % 2, (me // 2) % 2, (me // 4) % 2, me // 8
    to_y, to_x = me + 4 - 8 * y, me + 2 - 4 * x
    return dict(
        me=me, core=core, z=z, lines=n // 8,
        near=to_y * (1 - core) + to_x * core,
        far=to_x * (1 - core) + to_y * core,
        twin=me + 1 - 2 * core,
        i1=y * (1 - core) + x * core,
        i2=x * (1 - core) + y * core,
    )


def greet(at):
    barrier = pltpu.get_barrier_semaphore()
    z, lines = at["z"], at["lines"]

    def signal(device):
        pl.semaphore_signal(
            barrier, inc=1, device_id={"expert": device},
            device_id_type=pl.DeviceIdType.MESH,
        )

    for name in ("near", "far", "twin"):
        signal(at[name])

    @pl.when(z > 0)
    def _():
        signal(at["me"] - 8)

    @pl.when(z < lines - 1)
    def _():
        signal(at["me"] + 8)

    on_line = (z + lines - 1) // lines + (2 * lines - 2 - z) // lines
    pl.semaphore_wait(barrier, 3 + on_line)


def remote(src, dst, send_sem, recv_sem, device):
    return pltpu.make_async_remote_copy(
        src_ref=src, dst_ref=dst, send_sem=send_sem, recv_sem=recv_sem,
        device_id={"expert": device}, device_id_type=pl.DeviceIdType.MESH,
    )


def gather_kernel(n, own_ref, out_ref, send_sem, recv_sem, work=None, between=None):
    at = place(n)
    me, z, lines = at["me"], at["z"], at["lines"]
    near, far, twin = at["near"], at["far"], at["twin"]
    both = near + far - me
    greet(at)

    def send(kind, source, piece, device, begin, first=False):
        columns = span(piece, own_ref.shape[1])
        here = out_ref.at[source, :, columns]
        copy = remote(
            own_ref.at[:, columns] if first else here, here,
            send_sem.at[kind, source * PIECES + piece],
            recv_sem.at[source * PIECES + piece], device,
        )
        if begin:
            copy.start()
        else:
            copy.wait_send()

    def arrived_piece(source, piece):
        here = out_ref.at[source, :, span(piece, own_ref.shape[1])]
        remote(
            here, here, send_sem.at[0, source * PIECES + piece],
            recv_sem.at[source * PIECES + piece], twin,
        ).wait_recv()

    def arrived(source):
        for piece in range(PIECES):
            arrived_piece(source, piece)

    def line_sends(source, begin, up, down, first=False):
        for piece in range(PIECES):
            if begin and not first:
                arrived_piece(source, piece)
            if up:
                @pl.when(z < lines - 1)
                def _():
                    send(0, source, piece, me + 8, begin, first)
            if down:
                @pl.when(z > 0)
                def _():
                    send(1, source, piece, me - 8, begin, first)
            send(2, source, piece, near, begin, first)
            send(3, source, piece, far, begin, first)
            send(4, source, piece, twin, begin, first)

    def line_step(k, begin):
        @pl.when(z >= k)
        def _():
            line_sends(me - 8 * k, begin, True, False)

        @pl.when(z + k < lines)
        def _():
            line_sends(me + 8 * k, begin, False, True)

    def side_step(base, k, to_far, begin):
        def one(source):
            for piece in range(PIECES):
                if begin:
                    arrived_piece(source, piece)
                if to_far:
                    send(3, source, piece, far, begin)
                send(4, source, piece, twin, begin)

        if k == 0:
            one(base)
            return

        @pl.when(z >= k)
        def _():
            one(base - 8 * k)

        @pl.when(z + k < lines)
        def _():
            one(base + 8 * k)

    line_sends(me, True, True, True, True)
    out_ref[me] = own_ref[...]
    def twins_arrived(group):
        for line in range(lines):
            arrived(group + 8 * line + 1 - at["core"])

    def work_on(*devices):
        groups = [device - at["core"] - 8 * z for device in devices]
        for group in groups:
            twins_arrived(group)
        if work is not None:
            work(groups)

    for k in range(1, lines + 1):
        if k < lines:
            line_step(k, True)
        side_step(near, k - 1, True, True)
    for k in range(lines):
        side_step(far, k, False, True)
    work_on(me, near)
    for k in range(lines):
        side_step(both, k, False, True)
    work_on(far)
    if between is not None:
        between()
    work_on(both)
    line_sends(me, False, True, True, True)
    for k in range(lines):
        if k > 0:
            line_step(k, False)
        side_step(near, k, True, False)
        side_step(far, k, False, False)
        side_step(both, k, False, False)


def scatter_kernel(
    n, part_ref, *refs
):
    at = place(n)
    greet(at)
    start_twins, far_sends, finish = scatter_pieces(n, part_ref, *refs)
    near, far, me = at["near"], at["far"], at["me"]
    for device in (near + far - me, far, near, me):
        start_twins(device - at["core"] - 8 * at["z"])
    far_sends(False)
    far_sends(True)
    finish()


def scatter_pieces(
    n, part_ref, out_ref, twin_in, far_in, near_in, down_in, up_in, out_far, out_near, out_line,
    twin_send, twin_recv, far_send, far_recv, near_send, near_recv,
    down_send, down_recv, up_send, up_recv,
):
    at = place(n)
    me, z, lines, core = at["me"], at["z"], at["lines"], at["core"]
    near, far, twin, i1, i2 = at["near"], at["far"], at["twin"], at["i1"], at["i2"]
    order = []
    for step in range((lines + 1) // 2):
        order.append(step)
        if lines - 1 - step != step:
            order.append(lines - 1 - step)

    def chip(line, j1, j2, c):
        m1 = 2 - c
        m2 = 1 + c
        return line * 4 + j1 * m1 + j2 * m2

    def f32(value):
        return value.astype(jnp.float32)

    def moved(source, target, sems, slot, piece, device):
        columns = span(piece, part_ref.shape[2])
        send_sem, recv_sem = sems
        at_sem = slot * PIECES + piece
        return remote(
            source.at[:, columns], target.at[slot, :, columns],
            send_sem.at[at_sem], recv_sem.at[at_sem], device,
        )

    pieces = range(PIECES)

    def to_twin(slot, piece):
        source = part_ref.at[2 * slot + 1 - core]
        return moved(source, twin_in, (twin_send, twin_recv), slot, piece, twin)

    def start_twins(group):
        for line in order:
            for piece in pieces:
                to_twin(group // 2 + 4 * line, piece).start()

    def pair(line, j1, j2, piece):
        columns = span(piece, part_ref.shape[2])
        slot = chip(line, j1, j2, core)
        moved(
            twin_in.at[slot], twin_in, (twin_send, twin_recv), slot, piece, twin
        ).wait_recv()
        return f32(part_ref[2 * slot + core, :, columns]) + f32(twin_in[slot, :, columns])

    def to_far(line, j1, piece):
        slot = line * 2 + j1
        return moved(out_far.at[slot], far_in, (far_send, far_recv), slot, piece, far)

    def to_near(line, piece):
        return moved(out_near.at[line], near_in, (near_send, near_recv), line, piece, near)

    def to_down(line, piece):
        return moved(out_line.at[line], down_in, (down_send, down_recv), line, piece, me - 8)

    def to_up(line, piece):
        return moved(out_line.at[line], up_in, (up_send, up_recv), line, piece, me + 8)

    def far_sends(both):
        j1 = 1 - i1 if both else i1
        for line in order:
            for piece in pieces:
                columns = span(piece, part_ref.shape[2])
                value = pair(line, j1, 1 - i2, piece)
                out_far[line * 2 + j1, :, columns] = value.astype(jnp.bfloat16)
                to_far(line, j1, piece).start()

    def after_far(line, j1, piece):
        value = pair(line, j1, i2, piece)
        to_far(line, j1, piece).wait_recv()
        return value + f32(far_in[line * 2 + j1, :, span(piece, part_ref.shape[2])])

    def after_near(line, piece):
        value = after_far(line, i1, piece)
        to_near(line, piece).wait_recv()
        return value + f32(near_in[line, :, span(piece, part_ref.shape[2])])

    def line_sends(line, piece, begin):
        columns = span(piece, part_ref.shape[2])

        def one(copy, edge, landed):
            value = after_near(line, piece)

            @pl.when(edge)
            def _():
                out_line[line, :, columns] = value.astype(jnp.bfloat16)

            @pl.when(jnp.logical_not(edge))
            def _():
                copy.wait_recv()
                total = value + f32(landed[line, :, columns])
                out_line[line, :, columns] = total.astype(jnp.bfloat16)

            copy.start()

        @pl.when(z > line)
        def _():
            if begin:
                one(to_down(line, piece), z == lines - 1, down_in)
            else:
                to_down(line, piece).wait_send()

        @pl.when(z < line)
        def _():
            if begin:
                one(to_up(line, piece), z == 0, up_in)
            else:
                to_up(line, piece).wait_send()

    def finish():
        for line in order:
            for piece in pieces:
                columns = span(piece, part_ref.shape[2])
                value = after_far(line, 1 - i1, piece)
                out_near[line, :, columns] = value.astype(jnp.bfloat16)
                to_near(line, piece).start()
        for line in order:
            for piece in pieces:
                line_sends(line, piece, True)
        for piece in pieces:
            columns = span(piece, part_ref.shape[2])
            final = after_near(z, piece)

            @pl.when(z == 0)
            def _():
                to_down(z, piece).wait_recv()
                out_ref[:, columns] = (final + f32(down_in[z, :, columns])).astype(jnp.bfloat16)

            @pl.when(z == lines - 1)
            def _():
                to_up(z, piece).wait_recv()
                out_ref[:, columns] = (final + f32(up_in[z, :, columns])).astype(jnp.bfloat16)

            @pl.when((z > 0) & (z < lines - 1))
            def _():
                to_down(z, piece).wait_recv()
                to_up(z, piece).wait_recv()
                total = final + f32(down_in[z, :, columns]) + f32(up_in[z, :, columns])
                out_ref[:, columns] = total.astype(jnp.bfloat16)

        for line in range(lines):
            for piece in pieces:
                for j1 in range(2):
                    to_far(line, j1, piece).wait_send()
                    for j2 in range(2):
                        to_twin(4 * line + 2 * j1 + j2, piece).wait_send()
                to_near(line, piece).wait_send()
                line_sends(line, piece, False)

    return start_twins, far_sends, finish


def fused_kernel(
    n, own_ref, gate_hbm, up_hbm, down_hbm, out_ref,
    all_ref, part_ref, gate_ref, up_ref, down_ref, left_ref, act_ref, scale_ref,
    load_sem, send_sem, recv_sem, *refs
):
    at = place(n)
    lines = n // 8
    rows, features = part_ref.shape[1:]
    hidden = act_ref.shape[1]
    loads = [
        pltpu.make_async_copy(source, target, load_sem.at[i])
        for i, (source, target) in enumerate(
            ((gate_hbm, gate_ref), (up_hbm, up_ref), (down_hbm, down_ref))
        )
    ]
    for load in loads:
        load.start()
    start_twins, far_sends, finish = scatter_pieces(n, part_ref, out_ref, *refs)
    loaded = []

    def work(groups):
        if not loaded:
            for load in loads:
                load.wait()
            loaded.append(True)
        width = all_ref.shape[2] - features
        lane = lax.broadcasted_iota(jnp.int32, (rows, width), 1)
        own_expert = at["me"] // 2
        mine = (lane == own_expert) | (lane == own_expert + n // 2)
        places = [
            (group + 8 * line + core, ((order * lines + line) * 2 + core) * rows)
            for order, group in enumerate(groups) for line in range(lines) for core in range(2)
        ]
        total = len(places) * rows
        for index, base in places:
            left_ref[base:base + rows, :] = all_ref[index, :, :features]
            tail = all_ref[index, :, features:].astype(jnp.float32)
            scale = jnp.sum(jnp.where(mine, tail, 0.0), axis=1, keepdims=True)
            scale_ref[base:base + rows, :] = jnp.broadcast_to(scale, (rows, LANES))
        step = min(hidden, 2 * LANES)

        @pl.loop(0, hidden // step)
        def _(tile):
            columns = pl.ds(pl.multiple_of(tile * step, step), step)
            gate = jnp.dot(
                left_ref[:total, :], gate_ref[:, columns], preferred_element_type=jnp.float32
            )
            up = jnp.dot(
                left_ref[:total, :], up_ref[:, columns], preferred_element_type=jnp.float32
            )
            act_ref[:total, columns] = (gate / (1.0 + jnp.exp(-gate)) * up).astype(jnp.bfloat16)

        wide = min(features, 4 * LANES)

        @pl.loop(0, features // wide)
        def _(tile):
            columns = pl.ds(pl.multiple_of(tile * wide, wide), wide)
            part = jnp.dot(
                act_ref[:total, :], down_ref[:, columns], preferred_element_type=jnp.float32
            )
            part = (part * scale_ref[:total, :1]).astype(jnp.bfloat16)
            for index, base in places:
                part_ref[index, :, columns] = part[base:base + rows, :]

        for group in groups:
            start_twins(group)

    gather_kernel(
        n, own_ref, all_ref, send_sem, recv_sem, work, lambda: far_sends(False)
    )
    far_sends(True)
    finish()


def fused(own, gate_weight, up_weight, down_weight, n):
    rows = own.shape[0]
    hidden, features = down_weight.shape
    lines = n // 8
    block = (rows, features)

    def room(*shape):
        return pltpu.VMEM(shape, jnp.bfloat16)

    arrays = [
        (n,) + own.shape, (n,) + block, gate_weight.shape, up_weight.shape, down_weight.shape,
        (lines * 6 * rows, features), (lines * 6 * rows, hidden),
    ]
    slots = [
        (count,) + block
        for count in (n // 2, 2 * lines, lines, lines, lines, 2 * lines, lines, lines)
    ]
    counts = [n // 2, n // 2, 2 * lines, 2 * lines] + [lines] * 6
    if sum(2 * math.prod(shape) for shape in arrays + slots) > 52 * 2**20:
        return None
    anywhere = pl.BlockSpec(memory_space=pl.ANY)
    return pl.pallas_call(
        functools.partial(fused_kernel, n),
        out_shape=jax.ShapeDtypeStruct(block, jnp.bfloat16),
        in_specs=[pl.BlockSpec(memory_space=pltpu.VMEM), anywhere, anywhere, anywhere],
        out_specs=pl.BlockSpec(memory_space=pltpu.VMEM),
        scratch_shapes=[room(*shape) for shape in arrays] + [
            pltpu.VMEM((lines * 6 * rows, LANES), jnp.float32),
            pltpu.SemaphoreType.DMA((3,)),
            pltpu.SemaphoreType.DMA((5, n * PIECES)), pltpu.SemaphoreType.DMA((n * PIECES,)),
        ] + [room(*shape) for shape in slots]
        + [pltpu.SemaphoreType.DMA((count * PIECES,)) for count in counts],
        compiler_params=pltpu.CompilerParams(
            collective_id=2, has_side_effects=True, vmem_limit_bytes=60 * 2**20
        ),
        name="fused",
    )(own, gate_weight, up_weight, down_weight)


def gather_rows(own, n):
    return pl.pallas_call(
        functools.partial(gather_kernel, n),
        out_shape=jax.ShapeDtypeStruct((n,) + own.shape, own.dtype),
        in_specs=[pl.BlockSpec(memory_space=pltpu.VMEM)],
        out_specs=pl.BlockSpec(memory_space=pltpu.VMEM),
        scratch_shapes=[pltpu.SemaphoreType.DMA((5, n * PIECES)), pltpu.SemaphoreType.DMA((n * PIECES,))],
        compiler_params=pltpu.CompilerParams(
            collective_id=0, has_side_effects=True, vmem_limit_bytes=60 * 2**20
        ),
        name="gather_rows",
    )(own)


def scatter_sums(parts, n):
    block = parts.shape[1:]
    lines = n // 8

    def room(count):
        return pltpu.VMEM((count,) + block, jnp.bfloat16)

    counts = [n // 2, n // 2, 2 * lines, 2 * lines] + [lines] * 6
    return pl.pallas_call(
        functools.partial(scatter_kernel, n),
        out_shape=jax.ShapeDtypeStruct(block, jnp.bfloat16),
        in_specs=[pl.BlockSpec(memory_space=pltpu.VMEM)],
        out_specs=pl.BlockSpec(memory_space=pltpu.VMEM),
        scratch_shapes=[
            room(n // 2), room(2 * lines), room(lines), room(lines), room(lines),
            room(2 * lines), room(lines), room(lines),
        ] + [pltpu.SemaphoreType.DMA((count * PIECES,)) for count in counts],
        compiler_params=pltpu.CompilerParams(
            collective_id=1, has_side_effects=True, vmem_limit_bytes=60 * 2**20
        ),
        name="scatter_sums",
    )(parts)


def dense_gates(id_block, code_block, expert_count):
    code_rows = code_block.astype(jnp.float32)
    weights = route_scale * code_rows / jnp.sum(code_rows, axis=-1, keepdims=True)
    hit = id_block[..., None] == jnp.arange(expert_count, dtype=jnp.int32)
    return jnp.sum(jnp.where(hit, weights[..., None], 0.0), axis=-2)


def shards(hidden_rows, expert_ids, gate_codes, gate_weight, up_weight, down_weight):
    n = lax.axis_size("expert")
    expert_count = n // 2
    micro_count, rows_dev, feature_count = hidden_rows.shape
    block_rows = micro_count * rows_dev
    own_expert = lax.axis_index("expert") // 2
    gates = dense_gates(expert_ids, gate_codes, expert_count).reshape(block_rows, expert_count)
    high = lax.reduce_precision(gates, 8, 7)
    width = -(-2 * expert_count // LANES) * LANES
    tail = jnp.concatenate([high, gates - high], axis=1).astype(jnp.bfloat16)
    tail = jnp.pad(tail, ((0, 0), (0, width - 2 * expert_count)))
    own = jnp.concatenate([hidden_rows.reshape(block_rows, feature_count), tail], axis=1)
    combined = fused(own, gate_weight, up_weight, down_weight, n)
    if combined is not None:
        return combined.reshape(micro_count, rows_dev, feature_count)
    gathered = gather_rows(own, n).reshape(n * block_rows, feature_count + width)
    all_rows = gathered[:, :feature_count]
    tails = gathered[:, feature_count:].astype(jnp.float32)
    lane = jnp.arange(width, dtype=jnp.int32)
    mine = (lane == own_expert) | (lane == own_expert + expert_count)
    own_gate = jnp.sum(jnp.where(mine, tails, 0.0), axis=1, keepdims=True)
    gate_value = jnp.dot(all_rows, gate_weight, preferred_element_type=jnp.float32)
    up_value = jnp.dot(all_rows, up_weight, preferred_element_type=jnp.float32)
    hidden = (jax.nn.silu(gate_value) * up_value).astype(jnp.bfloat16)
    produced = jnp.dot(hidden, down_weight, preferred_element_type=jnp.float32)
    weighted = (produced * own_gate).astype(jnp.bfloat16)
    combined = scatter_sums(weighted.reshape(n, block_rows, feature_count), n)
    return combined.reshape(micro_count, rows_dev, feature_count)


def solution(mesh):
    return jax.shard_map(
        shards,
        mesh=mesh,
        in_specs=(
            P(None, ("groups", "expert"), None),
            P(None, ("groups", "expert"), None),
            P(None, ("groups", "expert"), None),
            P(None, "expert"),
            P(None, "expert"),
            P("expert", None),
        ),
        out_specs=P(None, ("groups", "expert"), None),
        check_vma=False,
    )
```

```python
import functools
import math

import jax
import jax.numpy as jnp
from jax import lax
from jax.experimental import pallas as pl
from jax.experimental.pallas import tpu as pltpu
from jax.sharding import PartitionSpec as P

route_scale = 2.5
LANES = 128
PIECES = 1


def span(piece, size):
    step = size // PIECES // LANES * LANES
    return slice(piece * step, size if piece == PIECES - 1 else (piece + 1) * step)


def place(n):
    me = lax.axis_index("expert")
    core, x, y, z = me % 2, (me // 2) % 2, (me // 4) % 2, me // 8
    to_y, to_x = me + 4 - 8 * y, me + 2 - 4 * x
    return dict(
        me=me, core=core, z=z, lines=n // 8,
        near=to_y * (1 - core) + to_x * core,
        far=to_x * (1 - core) + to_y * core,
        twin=me + 1 - 2 * core,
        i1=y * (1 - core) + x * core,
        i2=x * (1 - core) + y * core,
    )


def greet(at):
    barrier = pltpu.get_barrier_semaphore()
    z, lines = at["z"], at["lines"]

    def signal(device):
        pl.semaphore_signal(
            barrier, inc=1, device_id={"expert": device},
            device_id_type=pl.DeviceIdType.MESH,
        )

    for name in ("near", "far", "twin"):
        signal(at[name])

    @pl.when(z > 0)
    def _():
        signal(at["me"] - 8)

    @pl.when(z < lines - 1)
    def _():
        signal(at["me"] + 8)

    on_line = (z + lines - 1) // lines + (2 * lines - 2 - z) // lines
    pl.semaphore_wait(barrier, 3 + on_line)


def remote(src, dst, send_sem, recv_sem, device):
    return pltpu.make_async_remote_copy(
        src_ref=src, dst_ref=dst, send_sem=send_sem, recv_sem=recv_sem,
        device_id={"expert": device}, device_id_type=pl.DeviceIdType.MESH,
    )


def gather_kernel(n, own_ref, out_ref, send_sem, recv_sem, work=None, between=None):
    at = place(n)
    me, z, lines = at["me"], at["z"], at["lines"]
    near, far, twin = at["near"], at["far"], at["twin"]
    both = near + far - me
    greet(at)

    def send(kind, source, piece, device, begin, first=False):
        columns = span(piece, own_ref.shape[1])
        here = out_ref.at[source, :, columns]
        copy = remote(
            own_ref.at[:, columns] if first else here, here,
            send_sem.at[kind, source * PIECES + piece],
            recv_sem.at[source * PIECES + piece], device,
        )
        if begin:
            copy.start()
        else:
            copy.wait_send()

    def arrived_piece(source, piece):
        here = out_ref.at[source, :, span(piece, own_ref.shape[1])]
        remote(
            here, here, send_sem.at[0, source * PIECES + piece],
            recv_sem.at[source * PIECES + piece], twin,
        ).wait_recv()

    def arrived(source):
        for piece in range(PIECES):
            arrived_piece(source, piece)

    def line_sends(source, begin, up, down, first=False):
        for piece in range(PIECES):
            if begin and not first:
                arrived_piece(source, piece)
            if up:
                @pl.when(z < lines - 1)
                def _():
                    send(0, source, piece, me + 8, begin, first)
            if down:
                @pl.when(z > 0)
                def _():
                    send(1, source, piece, me - 8, begin, first)
            send(2, source, piece, near, begin, first)
            send(3, source, piece, far, begin, first)
            send(4, source, piece, twin, begin, first)

    def line_step(k, begin):
        @pl.when(z >= k)
        def _():
            line_sends(me - 8 * k, begin, True, False)

        @pl.when(z + k < lines)
        def _():
            line_sends(me + 8 * k, begin, False, True)

    def side_step(base, k, to_far, begin):
        def one(source):
            for piece in range(PIECES):
                if begin:
                    arrived_piece(source, piece)
                if to_far:
                    send(3, source, piece, far, begin)
                send(4, source, piece, twin, begin)

        if k == 0:
            one(base)
            return

        @pl.when(z >= k)
        def _():
            one(base - 8 * k)

        @pl.when(z + k < lines)
        def _():
            one(base + 8 * k)

    line_sends(me, True, True, True, True)
    out_ref[me] = own_ref[...]
    def twins_arrived(group):
        for line in range(lines):
            arrived(group + 8 * line + 1 - at["core"])

    def work_on(*devices):
        groups = [device - at["core"] - 8 * z for device in devices]
        for group in groups:
            twins_arrived(group)
        if work is not None:
            work(groups)

    for k in range(1, lines + 1):
        if k < lines:
            line_step(k, True)
        side_step(near, k - 1, True, True)
    for k in range(lines):
        side_step(far, k, False, True)
    work_on(me, near)
    for k in range(lines):
        side_step(both, k, False, True)
    work_on(far)
    if between is not None:
        between()
    work_on(both)
    line_sends(me, False, True, True, True)
    for k in range(lines):
        if k > 0:
            line_step(k, False)
        side_step(near, k, True, False)
        side_step(far, k, False, False)
        side_step(both, k, False, False)


def scatter_kernel(
    n, part_ref, *refs
):
    at = place(n)
    greet(at)
    start_twins, far_sends, finish = scatter_pieces(n, part_ref, *refs)
    near, far, me = at["near"], at["far"], at["me"]
    for device in (near + far - me, far, near, me):
        start_twins(device - at["core"] - 8 * at["z"])
    far_sends(False)
    far_sends(True)
    finish()


def scatter_pieces(
    n, part_ref, out_ref, twin_in, far_in, near_in, down_in, up_in, out_far, out_near, out_line,
    twin_send, twin_recv, far_send, far_recv, near_send, near_recv,
    down_send, down_recv, up_send, up_recv,
):
    at = place(n)
    me, z, lines, core = at["me"], at["z"], at["lines"], at["core"]
    near, far, twin, i1, i2 = at["near"], at["far"], at["twin"], at["i1"], at["i2"]
    order = []
    for step in range((lines + 1) // 2):
        order.append(step)
        if lines - 1 - step != step:
            order.append(lines - 1 - step)

    def chip(line, j1, j2, c):
        m1 = 2 - c
        m2 = 1 + c
        return line * 4 + j1 * m1 + j2 * m2

    def f32(value):
        return value.astype(jnp.float32)

    def moved(source, target, sems, slot, piece, device):
        columns = span(piece, part_ref.shape[2])
        send_sem, recv_sem = sems
        at_sem = slot * PIECES + piece
        return remote(
            source.at[:, columns], target.at[slot, :, columns],
            send_sem.at[at_sem], recv_sem.at[at_sem], device,
        )

    pieces = range(PIECES)

    def to_twin(slot, piece):
        source = part_ref.at[2 * slot + 1 - core]
        return moved(source, twin_in, (twin_send, twin_recv), slot, piece, twin)

    def start_twins(group):
        for line in order:
            for piece in pieces:
                to_twin(group // 2 + 4 * line, piece).start()

    def pair(line, j1, j2, piece):
        columns = span(piece, part_ref.shape[2])
        slot = chip(line, j1, j2, core)
        moved(
            twin_in.at[slot], twin_in, (twin_send, twin_recv), slot, piece, twin
        ).wait_recv()
        return f32(part_ref[2 * slot + core, :, columns]) + f32(twin_in[slot, :, columns])

    def to_far(line, j1, piece):
        slot = line * 2 + j1
        return moved(out_far.at[slot], far_in, (far_send, far_recv), slot, piece, far)

    def to_near(line, piece):
        return moved(out_near.at[line], near_in, (near_send, near_recv), line, piece, near)

    def to_down(line, piece):
        return moved(out_line.at[line], down_in, (down_send, down_recv), line, piece, me - 8)

    def to_up(line, piece):
        return moved(out_line.at[line], up_in, (up_send, up_recv), line, piece, me + 8)

    def far_sends(both):
        j1 = 1 - i1 if both else i1
        for line in order:
            for piece in pieces:
                columns = span(piece, part_ref.shape[2])
                value = pair(line, j1, 1 - i2, piece)
                out_far[line * 2 + j1, :, columns] = value.astype(jnp.bfloat16)
                to_far(line, j1, piece).start()

    def after_far(line, j1, piece):
        value = pair(line, j1, i2, piece)
        to_far(line, j1, piece).wait_recv()
        return value + f32(far_in[line * 2 + j1, :, span(piece, part_ref.shape[2])])

    def after_near(line, piece):
        value = after_far(line, i1, piece)
        to_near(line, piece).wait_recv()
        return value + f32(near_in[line, :, span(piece, part_ref.shape[2])])

    def line_sends(line, piece, begin):
        columns = span(piece, part_ref.shape[2])

        def one(copy, edge, landed):
            value = after_near(line, piece)

            @pl.when(edge)
            def _():
                out_line[line, :, columns] = value.astype(jnp.bfloat16)

            @pl.when(jnp.logical_not(edge))
            def _():
                copy.wait_recv()
                total = value + f32(landed[line, :, columns])
                out_line[line, :, columns] = total.astype(jnp.bfloat16)

            copy.start()

        @pl.when(z > line)
        def _():
            if begin:
                one(to_down(line, piece), z == lines - 1, down_in)
            else:
                to_down(line, piece).wait_send()

        @pl.when(z < line)
        def _():
            if begin:
                one(to_up(line, piece), z == 0, up_in)
            else:
                to_up(line, piece).wait_send()

    def finish():
        for line in order:
            for piece in pieces:
                columns = span(piece, part_ref.shape[2])
                value = after_far(line, 1 - i1, piece)
                out_near[line, :, columns] = value.astype(jnp.bfloat16)
                to_near(line, piece).start()
        for line in order:
            for piece in pieces:
                line_sends(line, piece, True)
        for piece in pieces:
            columns = span(piece, part_ref.shape[2])
            final = after_near(z, piece)

            @pl.when(z == 0)
            def _():
                to_down(z, piece).wait_recv()
                out_ref[:, columns] = (final + f32(down_in[z, :, columns])).astype(jnp.bfloat16)

            @pl.when(z == lines - 1)
            def _():
                to_up(z, piece).wait_recv()
                out_ref[:, columns] = (final + f32(up_in[z, :, columns])).astype(jnp.bfloat16)

            @pl.when((z > 0) & (z < lines - 1))
            def _():
                to_down(z, piece).wait_recv()
                to_up(z, piece).wait_recv()
                total = final + f32(down_in[z, :, columns]) + f32(up_in[z, :, columns])
                out_ref[:, columns] = total.astype(jnp.bfloat16)

        for line in range(lines):
            for piece in pieces:
                for j1 in range(2):
                    to_far(line, j1, piece).wait_send()
                    for j2 in range(2):
                        to_twin(4 * line + 2 * j1 + j2, piece).wait_send()
                to_near(line, piece).wait_send()
                line_sends(line, piece, False)

    return start_twins, far_sends, finish


def fused_kernel(
    n, own_ref, gate_hbm, up_hbm, down_hbm, out_ref,
    all_ref, part_ref, gate_ref, up_ref, down_ref, left_ref, act_ref, scale_ref,
    load_sem, send_sem, recv_sem, *refs
):
    at = place(n)
    lines = n // 8
    rows, features = part_ref.shape[1:]
    hidden = act_ref.shape[1]
    loads = [
        pltpu.make_async_copy(source, target, load_sem.at[i])
        for i, (source, target) in enumerate(
            ((gate_hbm, gate_ref), (up_hbm, up_ref), (down_hbm, down_ref))
        )
    ]
    for load in loads:
        load.start()
    start_twins, far_sends, finish = scatter_pieces(n, part_ref, out_ref, *refs)
    loaded = []

    def work(groups):
        if not loaded:
            for load in loads:
                load.wait()
            loaded.append(True)
        width = all_ref.shape[2] - features
        lane = lax.broadcasted_iota(jnp.int32, (rows, width), 1)
        own_expert = at["me"] // 2
        mine = (lane == own_expert) | (lane == own_expert + n // 2)
        places = [
            (group + 8 * line + core, ((order * lines + line) * 2 + core) * rows)
            for order, group in enumerate(groups) for line in range(lines) for core in range(2)
        ]
        total = len(places) * rows
        for index, base in places:
            left_ref[base:base + rows, :] = all_ref[index, :, :features]
            tail = all_ref[index, :, features:].astype(jnp.float32)
            scale = jnp.sum(jnp.where(mine, tail, 0.0), axis=1, keepdims=True)
            scale_ref[base:base + rows, :] = jnp.broadcast_to(scale, (rows, LANES))
        step = min(hidden, 2 * LANES)

        @pl.loop(0, hidden // step)
        def _(tile):
            columns = pl.ds(pl.multiple_of(tile * step, step), step)
            gate = jnp.dot(
                left_ref[:total, :], gate_ref[:, columns], preferred_element_type=jnp.float32
            )
            up = jnp.dot(
                left_ref[:total, :], up_ref[:, columns], preferred_element_type=jnp.float32
            )
            act_ref[:total, columns] = (gate / (1.0 + jnp.exp(-gate)) * up).astype(jnp.bfloat16)

        wide = min(features, 8 * LANES)

        @pl.loop(0, features // wide)
        def _(tile):
            columns = pl.ds(pl.multiple_of(tile * wide, wide), wide)
            part = jnp.dot(
                act_ref[:total, :], down_ref[:, columns], preferred_element_type=jnp.float32
            )
            part = (part * scale_ref[:total, :1]).astype(jnp.bfloat16)
            for index, base in places:
                part_ref[index, :, columns] = part[base:base + rows, :]

        for group in groups:
            start_twins(group)

    gather_kernel(
        n, own_ref, all_ref, send_sem, recv_sem, work, lambda: far_sends(False)
    )
    far_sends(True)
    finish()


def fused(own, gate_weight, up_weight, down_weight, n):
    rows = own.shape[0]
    hidden, features = down_weight.shape
    lines = n // 8
    block = (rows, features)

    def room(*shape):
        return pltpu.VMEM(shape, jnp.bfloat16)

    arrays = [
        (n,) + own.shape, (n,) + block, gate_weight.shape, up_weight.shape, down_weight.shape,
        (lines * 6 * rows, features), (lines * 6 * rows, hidden),
    ]
    slots = [
        (count,) + block
        for count in (n // 2, 2 * lines, lines, lines, lines, 2 * lines, lines, lines)
    ]
    counts = [n // 2, n // 2, 2 * lines, 2 * lines] + [lines] * 6
    if sum(2 * math.prod(shape) for shape in arrays + slots) > 52 * 2**20:
        return None
    anywhere = pl.BlockSpec(memory_space=pl.ANY)
    return pl.pallas_call(
        functools.partial(fused_kernel, n),
        out_shape=jax.ShapeDtypeStruct(block, jnp.bfloat16),
        in_specs=[pl.BlockSpec(memory_space=pltpu.VMEM), anywhere, anywhere, anywhere],
        out_specs=pl.BlockSpec(memory_space=pltpu.VMEM),
        scratch_shapes=[room(*shape) for shape in arrays] + [
            pltpu.VMEM((lines * 6 * rows, LANES), jnp.float32),
            pltpu.SemaphoreType.DMA((3,)),
            pltpu.SemaphoreType.DMA((5, n * PIECES)), pltpu.SemaphoreType.DMA((n * PIECES,)),
        ] + [room(*shape) for shape in slots]
        + [pltpu.SemaphoreType.DMA((count * PIECES,)) for count in counts],
        compiler_params=pltpu.CompilerParams(
            collective_id=2, has_side_effects=True, vmem_limit_bytes=60 * 2**20
        ),
        name="fused",
    )(own, gate_weight, up_weight, down_weight)


def gather_rows(own, n):
    return pl.pallas_call(
        functools.partial(gather_kernel, n),
        out_shape=jax.ShapeDtypeStruct((n,) + own.shape, own.dtype),
        in_specs=[pl.BlockSpec(memory_space=pltpu.VMEM)],
        out_specs=pl.BlockSpec(memory_space=pltpu.VMEM),
        scratch_shapes=[pltpu.SemaphoreType.DMA((5, n * PIECES)), pltpu.SemaphoreType.DMA((n * PIECES,))],
        compiler_params=pltpu.CompilerParams(
            collective_id=0, has_side_effects=True, vmem_limit_bytes=60 * 2**20
        ),
        name="gather_rows",
    )(own)


def scatter_sums(parts, n):
    block = parts.shape[1:]
    lines = n // 8

    def room(count):
        return pltpu.VMEM((count,) + block, jnp.bfloat16)

    counts = [n // 2, n // 2, 2 * lines, 2 * lines] + [lines] * 6
    return pl.pallas_call(
        functools.partial(scatter_kernel, n),
        out_shape=jax.ShapeDtypeStruct(block, jnp.bfloat16),
        in_specs=[pl.BlockSpec(memory_space=pltpu.VMEM)],
        out_specs=pl.BlockSpec(memory_space=pltpu.VMEM),
        scratch_shapes=[
            room(n // 2), room(2 * lines), room(lines), room(lines), room(lines),
            room(2 * lines), room(lines), room(lines),
        ] + [pltpu.SemaphoreType.DMA((count * PIECES,)) for count in counts],
        compiler_params=pltpu.CompilerParams(
            collective_id=1, has_side_effects=True, vmem_limit_bytes=60 * 2**20
        ),
        name="scatter_sums",
    )(parts)


def dense_gates(id_block, code_block, expert_count):
    code_rows = code_block.astype(jnp.float32)
    weights = route_scale * code_rows / jnp.sum(code_rows, axis=-1, keepdims=True)
    hit = id_block[..., None] == jnp.arange(expert_count, dtype=jnp.int32)
    return jnp.sum(jnp.where(hit, weights[..., None], 0.0), axis=-2)


def shards(hidden_rows, expert_ids, gate_codes, gate_weight, up_weight, down_weight):
    n = lax.axis_size("expert")
    expert_count = n // 2
    micro_count, rows_dev, feature_count = hidden_rows.shape
    block_rows = micro_count * rows_dev
    own_expert = lax.axis_index("expert") // 2
    gates = dense_gates(expert_ids, gate_codes, expert_count).reshape(block_rows, expert_count)
    high = lax.reduce_precision(gates, 8, 7)
    width = -(-2 * expert_count // LANES) * LANES
    tail = jnp.concatenate([high, gates - high], axis=1).astype(jnp.bfloat16)
    tail = jnp.pad(tail, ((0, 0), (0, width - 2 * expert_count)))
    own = jnp.concatenate([hidden_rows.reshape(block_rows, feature_count), tail], axis=1)
    combined = fused(own, gate_weight, up_weight, down_weight, n)
    if combined is not None:
        return combined.reshape(micro_count, rows_dev, feature_count)
    gathered = gather_rows(own, n).reshape(n * block_rows, feature_count + width)
    all_rows = gathered[:, :feature_count]
    tails = gathered[:, feature_count:].astype(jnp.float32)
    lane = jnp.arange(width, dtype=jnp.int32)
    mine = (lane == own_expert) | (lane == own_expert + expert_count)
    own_gate = jnp.sum(jnp.where(mine, tails, 0.0), axis=1, keepdims=True)
    gate_value = jnp.dot(all_rows, gate_weight, preferred_element_type=jnp.float32)
    up_value = jnp.dot(all_rows, up_weight, preferred_element_type=jnp.float32)
    hidden = (jax.nn.silu(gate_value) * up_value).astype(jnp.bfloat16)
    produced = jnp.dot(hidden, down_weight, preferred_element_type=jnp.float32)
    weighted = (produced * own_gate).astype(jnp.bfloat16)
    combined = scatter_sums(weighted.reshape(n, block_rows, feature_count), n)
    return combined.reshape(micro_count, rows_dev, feature_count)


def solution(mesh):
    return jax.shard_map(
        shards,
        mesh=mesh,
        in_specs=(
            P(None, ("groups", "expert"), None),
            P(None, ("groups", "expert"), None),
            P(None, ("groups", "expert"), None),
            P(None, "expert"),
            P(None, "expert"),
            P("expert", None),
        ),
        out_specs=P(None, ("groups", "expert"), None),
        check_vma=False,
    )
```
